32 devices in a mesh: dp: 8 (over z, y), rep: 4 (over x, core).
Axes of the slice: x: 2, y: 2, z: 4, core: 2. Of those that a mesh axis runs over, the one named last changes fastest.
Arguments:
- block_in: bfloat16 [4, 12288, 2048], P('rep', 'dp')
- crop_codes: int32 [4, 1, 96], P('rep'), may hold values from 0 to 4, as said below
- tile_perm: int32 [4, 1, 768], P('rep'), may hold values from 0 to 767, each once within a row
- reduce_weight: bfloat16 [2048, 512], replicated, may hold values from -0.125 to 0.125
- dilated_weight: bfloat16 [4608, 512], replicated, may hold values from -0.09375 to 0.09375
- expand_weight: bfloat16 [512, 2048], replicated, may hold values from -0.25 to 0.25
- first_gain: float32 [512], replicated, may hold values from 0.5 to 1.5
- first_bias: float32 [512], replicated, may hold values from -1.5 to 1.5
- middle_gain: float32 [512], replicated, may hold values from 0.5 to 1.5
- middle_bias: float32 [512], replicated, may hold values from -1.5 to 1.5
- last_gain: float32 [2048], replicated, may hold values from 0.5 to 1.5
- last_bias: float32 [2048], replicated, may hold values from -1.5 to 1.5
- cotangent: bfloat16 [4, 12288, 2048], P('rep', 'dp'), may hold values from -6 to 6
Outputs:
- block_out: bfloat16 [4, 12288, 2048], P('rep', 'dp')
- grad_in: float32 [4, 12288, 2048], P('rep', 'dp')
- reduce_grad: float32 [2048, 512], replicated
- dilated_grad: float32 [4608, 512], replicated
- expand_grad: float32 [512, 2048], replicated
- first_gain_grad: float32 [512], replicated
- first_bias_grad: float32 [512], replicated
- middle_gain_grad: float32 [512], replicated
- middle_bias_grad: float32 [512], replicated
- last_gain_grad: float32 [2048], replicated
- final_bias_gradient: float32 [2048], replicated
The draws below stay inside these ranges and needn't reach their ends.
Inputs may be any that keep to these rules, and one draw needn't show every extreme that they name: `crop_codes`: in every group and set the first slot is 4, the tile counts 8 u u of the slots sum to exactly 768, and the slots after the last crop are 0. tile_perm[r, s] is a permutation.
All inputs are finite; a program needn't handle non-finite values.
Results may differ from the reference program's by a relative error of at most 0.012.
Values may be sent and summed in bfloat16 or wider, within the bound.
No kernel may reach another device: no remote copies, remote signals or barrier semaphores. Data moves between devices by JAX's collectives and lax.ppermute only.
A program may use at most 256 MiB of HBM per device.

```python
from functools import partial
import jax
import jax.numpy as jnp
from jax import lax

C = 2048
MID = 512
DILATION_RATE = 4
PIX_DEV = 1536
SETS = 1
TK = 96
TILES = 768
MAXC = 96
ROWS = 12288
TOTAL = 49152
N_REP = 4


def draw_block_in(key, part):
    first, second = jax.random.split(key, 2)
    shape = (N_REP, ROWS, C)
    position = (jnp.arange(N_REP, dtype=jnp.float32)[:, None] * ROWS + jnp.arange(ROWS, dtype=jnp.float32)[None, :]) / TOTAL
    rough = jnp.exp(jax.random.uniform(second, (N_REP, ROWS), minval=-0.35, maxval=0.35))
    scale = 0.3 * jnp.exp(2.302585 * position) * rough
    values = jnp.abs(jax.random.normal(first, shape))
    return (values * scale[:, :, None]).astype(jnp.float32).astype(jnp.bfloat16)


def draw_crop_codes(key, part):

    def one_set(set_key):
        slot_keys = jax.random.split(set_key, MAXC)

        def choose_slot(remaining, slot_key):
            choices = jnp.arange(1, 5, dtype=jnp.int32)
            allowed = jnp.sum((8 * choices * choices <= remaining).astype(jnp.int32), dtype=jnp.int32)
            picked = (jax.random.randint(slot_key, (), 0, 4, dtype=jnp.int32) % jnp.maximum(allowed, 1)).astype(jnp.int32) + 1
            chosen = jnp.where(allowed > 0, picked, 0).astype(jnp.int32)
            return ((remaining - 8 * chosen * chosen).astype(jnp.int32), chosen)
        _, others = lax.scan(choose_slot, jnp.int32(TILES - 128), slot_keys[1:])
        return jnp.concatenate([jnp.array([4], jnp.int32), others.astype(jnp.int32)])
    set_keys = jax.random.split(key, N_REP * SETS)
    return jax.vmap(one_set)(set_keys).reshape(N_REP, SETS, MAXC).astype(jnp.int32)


def block_scale(key, dims, pieces, least, top_value):
    def one(axis_at, shards_of):
        draws = jax.random.uniform(jax.random.fold_in(jax.random.fold_in(key, 6), axis_at), (shards_of,), jnp.float32, least / len(pieces), top_value / len(pieces))
        return jnp.repeat(jnp.exp(draws), dims[axis_at] // shards_of).reshape((-1,) + (1,) * (len(dims) - axis_at - 1))

    level = one(*pieces[0])
    for cut in pieces[1:]:
        level = level * one(*cut)
    return level


def scatter_about(own_key, shape, scale, limit, cuts=(), kind=jnp.bfloat16):
    entries = jax.random.normal(own_key, shape, jnp.float32) * scale
    if len(cuts) > 0:
        entries = block_scale(own_key, shape, cuts, -0.22, 0.18) * entries
    return jnp.clip(entries, min=-limit, max=limit).astype(kind)


def setup_inputs(seed: int = 0) -> dict:
    key_list = jax.random.split(jax.random.key(seed), 14)
    return {
        "block_in": draw_block_in(jax.random.fold_in(key_list[13], 71), 0),
        "crop_codes": draw_crop_codes(jax.random.fold_in(key_list[13], 71), 0),
        "tile_perm": jax.vmap(lambda own: jax.random.permutation(own, TILES))(jax.random.split(key_list[2], N_REP * SETS)).reshape((N_REP, SETS, TILES)).astype(jnp.int32),
        "reduce_weight": scatter_about(key_list[3], (C, MID), C ** -0.5, 0.125),
        "dilated_weight": scatter_about(key_list[4], (9 * MID, MID), (9 * MID) ** -0.5, 0.09375),
        "expand_weight": scatter_about(key_list[5], (MID, C), MID ** -0.5, 0.25),
        "first_gain": jnp.clip(1.0 + 0.1 * jax.random.normal(key_list[6], (MID,), jnp.float32), 0.5, 1.5),
        "first_bias": scatter_about(key_list[7], (MID,), 0.3, 1.5, (), jnp.float32),
        "middle_gain": jnp.clip(1.0 + 0.1 * jax.random.normal(key_list[8], (MID,), jnp.float32), 0.5, 1.5),
        "middle_bias": scatter_about(key_list[9], (MID,), 0.3, 1.5, (), jnp.float32),
        "last_gain": jnp.clip(1.0 + 0.1 * jax.random.normal(key_list[10], (C,), jnp.float32), 0.5, 1.5),
        "last_bias": scatter_about(key_list[11], (C,), 0.3, 1.5, (), jnp.float32),
        "cotangent": scatter_about(key_list[12], (N_REP, ROWS, C), 1.0, 6.0, ((0, 4), (1, 8))),
    }


EPS = 1e-05
HIGH = lax.Precision.HIGHEST

@jax.custom_vjp
def low(v):
    return lax.optimization_barrier(v.astype(jnp.bfloat16)).astype(jnp.float32)

@jax.custom_vjp
def low_back(v):
    return v

def low_keep(v):
    return (low(v), None)

def low_pass(kept, grad):
    return (grad,)

def back_keep(v):
    return (v, None)

def back_low(kept, grad):
    return (low(grad),)
low.defvjp(low_keep, low_pass)
low_back.defvjp(back_keep, back_low)

def crop_tables(codes, tiles):
    slots = codes.shape[0]
    sizes = (8 * codes * codes).astype(jnp.int32)
    ending = jnp.cumsum(sizes, dtype=jnp.int32)
    starting = ending - sizes
    number = jnp.arange(tiles, dtype=jnp.int32)
    owner = lax.optimization_barrier(jnp.sum((ending[None, :] <= number[:, None]).astype(jnp.int32), axis=1, dtype=jnp.int32))
    onehot = (owner[:, None] == jnp.arange(slots, dtype=jnp.int32)[None, :]).astype(jnp.int32)
    first = lax.optimization_barrier(jnp.sum(onehot * starting[None, :], axis=1, dtype=jnp.int32))
    scale = lax.optimization_barrier(jnp.sum(onehot * codes[None, :], axis=1, dtype=jnp.int32))
    width = 4 * scale
    height = 2 * scale
    local = number - first
    across = local // width
    along = local % width
    columns = []
    for shift_row in (-1, 0, 1):
        for shift_col in (-1, 0, 1):
            inside = (across + shift_row >= 0) & (across + shift_row < height) & (along + shift_col >= 0) & (along + shift_col < width)
            columns.append(jnp.where(inside, number + shift_row * width + shift_col, tiles).astype(jnp.int32))
    return jnp.stack(columns, axis=1).astype(jnp.int32)

def normalize(values):
    axes = tuple(range(values.ndim - 1))
    mean = lax.optimization_barrier(jnp.mean(values, axis=axes))
    spread = lax.optimization_barrier(jnp.mean(values * values, axis=axes)) - mean * mean
    return (values - mean) * lax.rsqrt(spread + EPS)

def reference(block_in, crop_codes, tile_perm, reduce_weight, dilated_weight, expand_weight, first_gain, first_bias, middle_gain, middle_bias, last_gain, last_bias, cotangent):
    groups = block_in.shape[0]
    group_rows = block_in.shape[1]
    middle = reduce_weight.shape[1]
    phase_groups = DILATION_RATE * DILATION_RATE
    neighbors = jax.vmap(jax.vmap(partial(crop_tables, tiles=TILES)))(crop_codes)
    inverse = jnp.argsort(tile_perm, axis=-1).astype(jnp.int32)
    holder = inverse // TK
    within = inverse % TK
    block_of = (jnp.arange(SETS, dtype=jnp.int32)[None, :, None, None] * phase_groups + jnp.arange(phase_groups, dtype=jnp.int32)[None, None, :, None]) * TK
    placed = holder[:, :, None, :] * PIX_DEV + block_of + within[:, :, None, :]
    order = placed.reshape(groups, group_rows).astype(jnp.int32)
    back = jnp.argsort(order, axis=1).astype(jnp.int32)

    def forward(inputs, w_first, w_middle, w_last, gain_one, bias_one, gain_two, bias_two, gain_three, bias_three):
        hidden_one = low_back(jnp.einsum('grc,cm->grm', inputs, w_first, precision=HIGH))
        act_one = low_back(low(jax.nn.silu(gain_one * normalize(hidden_one) + bias_one)))
        gathered = jnp.take_along_axis(act_one, order[:, :, None], axis=1).reshape(groups, SETS, phase_groups, TILES, middle)
        padded = jnp.concatenate([gathered, jnp.zeros((groups, SETS, phase_groups, 1, middle), jnp.float32)], axis=3)
        total = jnp.zeros((groups, SETS, phase_groups, TILES, middle), jnp.float32)
        for offset in range(9):
            picked = jnp.take_along_axis(padded, neighbors[:, :, None, :, offset, None], axis=3)
            total = total + jnp.einsum('gsptm,mn->gsptn', picked, w_middle[offset * middle:(offset + 1) * middle], precision=HIGH)
        hidden_two = low_back(total.reshape(groups, group_rows, middle))
        act_two = low_back(low(jax.nn.silu(gain_two * normalize(hidden_two) + bias_two)))
        natural = jnp.take_along_axis(act_two, back[:, :, None], axis=1)
        hidden_three = low_back(jnp.einsum('grm,mc->grc', natural, w_last, precision=HIGH))
        summed = gain_three * normalize(hidden_three) + bias_three + inputs
        return jax.nn.silu(summed)
    primal_inputs, pull = jax.vjp(forward, block_in.astype(jnp.float32), reduce_weight.astype(jnp.float32), dilated_weight.astype(jnp.float32), expand_weight.astype(jnp.float32), first_gain, first_bias, middle_gain, middle_bias, last_gain, last_bias)
    grads = pull(cotangent.astype(jnp.float32))
    return (primal_inputs.astype(jnp.bfloat16), grads[0], grads[1], grads[2], grads[3], grads[4], grads[5], grads[6], grads[7], grads[8], grads[9])
```

```python
import jax
import jax.numpy as jnp
from jax import lax
from jax.experimental import pallas as pl
from jax.experimental.pallas import tpu as pltpu
from jax.sharding import PartitionSpec as P

EPS = 1e-05
F32 = jnp.float32
BF16 = jnp.bfloat16
VMEM_BYTES = 58 * 1024 * 1024
BLOCKS = 8
AXES = ("dp", "rep")


def params(grid_rank=0):
    kwargs = {"vmem_limit_bytes": VMEM_BYTES}
    if grid_rank:
        kwargs["dimension_semantics"] = ("arbitrary",) * grid_rank
    return pltpu.CompilerParams(**kwargs)


def sigmoid(v):
    return 0.5 * jnp.tanh(0.5 * v) + 0.5


def dot(a, b, dims=((1,), (0,))):
    return lax.dot_general(a, b, (dims, ((), ())), preferred_element_type=F32)


def moments(sums, total):
    mean = sums[0:1] / total
    scale = lax.rsqrt(sums[1:2] / total - mean * mean + EPS)
    return mean, scale


def column_sums(a, b):
    return jnp.concatenate(
        [jnp.sum(a, axis=0, keepdims=True), jnp.sum(b, axis=0, keepdims=True)], axis=0
    )


def xor_blocks(values, me):
    for bit in range(3):
        paired = values.reshape((BLOCKS >> (bit + 1), 2, 1 << bit) + values.shape[1:])
        flipped = paired[:, ::-1].reshape(values.shape)
        values = jnp.where(((me >> bit) & 1) == 1, flipped, values)
    return values


def tile_table(codes, order, tiles):
    slots = codes.shape[0]
    sizes = 8 * codes * codes
    before = jnp.arange(slots)[:, None] <= jnp.arange(slots)[None, :]
    ending = jnp.sum(jnp.where(before, sizes[:, None], 0), axis=0, dtype=jnp.int32)
    number = jnp.arange(tiles, dtype=jnp.int32)
    started = (ending - sizes)[None, :] <= number[:, None]
    mine = started & (number[:, None] < ending[None, :])
    first = jnp.sum(jnp.where(mine, (ending - sizes)[None, :], 0), axis=1, dtype=jnp.int32)
    scale = jnp.sum(jnp.where(mine, codes[None, :], 0), axis=1, dtype=jnp.int32)
    width = 4 * scale
    height = 2 * scale
    local = number - first
    across = local // width
    along = local - across * width
    above = jnp.where(across > 0, number - width, -1)
    below = jnp.where(across < height - 1, number + width, -1)
    left = (along > 0).astype(jnp.int32)
    right = (along < width - 1).astype(jnp.int32)
    zero = jnp.zeros_like(number)
    return jnp.stack([above, number, below, left, right, order, zero, zero], axis=1)


def first_kernel(me_ref, x_ref, w_ref, *outs):
    step = pl.program_id(0)
    st_ref = outs[BLOCKS]
    h = dot(x_ref[0], w_ref[...])
    packed = h.astype(BF16)
    for k in range(BLOCKS):

        @pl.when(step == k)
        def _():
            outs[k][...] = packed

    part = column_sums(h, h * h)

    @pl.when(step == 0)
    def _():
        st_ref[...] = part

    @pl.when(step > 0)
    def _():
        st_ref[...] += part


def first_call(me, inputs, weight):
    rows, width = inputs.shape[1:]
    middle = weight.shape[1]
    whole = pl.BlockSpec((rows, middle), lambda b, me: (0, 0))
    return pl.pallas_call(
        first_kernel,
        grid_spec=pltpu.PrefetchScalarGridSpec(
            num_scalar_prefetch=1,
            grid=(BLOCKS,),
            in_specs=[
                pl.BlockSpec((1, rows, width), lambda b, me: (b ^ me[0], 0, 0)),
                pl.BlockSpec((width, middle), lambda b, me: (0, 0)),
            ],
            out_specs=[whole] * BLOCKS + [pl.BlockSpec((2, middle), lambda b, me: (0, 0))],
        ),
        out_shape=[jax.ShapeDtypeStruct((rows, middle), BF16)] * BLOCKS
        + [jax.ShapeDtypeStruct((2, middle), F32)],
        compiler_params=params(1),
        name="first_matmul",
    )(me, inputs, weight)


def side_mask(tab_ref, column, phases):
    mask = tab_ref[:, column : column + 1].astype(F32)
    return jnp.concatenate([mask] * phases, axis=0) if phases > 1 else mask


def onehot(column, row):
    return jnp.where(column == row, 1.0, 0.0).astype(BF16)


def shift_add(center, left, right, left_mask, right_mask):
    rows = center.shape[0]
    return (
        center
        + left_mask * pltpu.roll(left, 1, axis=0)
        + right_mask * pltpu.roll(right, rows - 1, axis=0)
    )


def conv_kernel(total, phases, nslots):
    def kernel(*refs):
        sums_ref, gain_ref, bias_ref, tab_ref, perm_ref, w_ref = refs[:6]
        slots = refs[6 : 6 + nslots]
        cols_ref, h_ref, st_ref = refs[6 + nslots : 9 + nslots]
        sends = refs[9 + nslots : 9 + 2 * nslots]
        act_ref = refs[9 + 2 * nslots]
        tiles = tab_ref.shape[0]
        each = tiles // nslots
        middle = h_ref.shape[1]
        mean, rs = moments(sums_ref[...], total)
        scale = gain_ref[...] * rs
        shift = bias_ref[...] - mean * scale
        for k in range(nslots):
            for j in range(phases):
                u = slots[k][j * each : (j + 1) * each, :].astype(F32) * scale + shift
                act_ref[k * each : (k + 1) * each, j * middle : (j + 1) * middle] = (
                    u * sigmoid(u)
                ).astype(BF16)
        row = perm_ref[...]
        for dy in range(3):
            picked = dot(onehot(tab_ref[:, dy : dy + 1], row), act_ref[...]).astype(BF16)
            for j in range(phases):
                cols_ref[j * tiles : (j + 1) * tiles, dy * middle : (dy + 1) * middle] = picked[
                    :, j * middle : (j + 1) * middle
                ]
        parts = [
            dot(cols_ref[...], w_ref[:, dx].reshape(3 * middle, middle)) for dx in range(3)
        ]
        h = shift_add(
            parts[1], parts[0], parts[2], side_mask(tab_ref, 3, phases), side_mask(tab_ref, 4, phases)
        )
        h_ref[...] = h
        st_ref[...] = column_sums(h, h * h)
        packed = h.astype(BF16)
        wide = (
            jnp.concatenate([packed[j * tiles : (j + 1) * tiles] for j in range(phases)], axis=1)
            if phases > 1
            else packed
        )
        scatter(tab_ref, wide, sends, phases)

    return kernel


def scatter(tab_ref, wide, sends, phases):
    tiles = tab_ref.shape[0]
    each = tiles // len(sends)
    middle = wide.shape[1] // phases
    row = lax.broadcasted_iota(jnp.int32, (1, tiles), 1)
    back = dot(onehot(tab_ref[:, 5:6], row), wide).astype(BF16)
    for k, send in enumerate(sends):
        for j in range(phases):
            send[j * each : (j + 1) * each, :] = back[
                k * each : (k + 1) * each, j * middle : (j + 1) * middle
            ]


def conv_call(total, phases, sums, gain, bias, table, perm, weight, slots):
    tiles = table.shape[0]
    middle = weight.shape[-1]
    n = len(slots)
    rows = phases * tiles
    slot = jax.ShapeDtypeStruct((rows // n, middle), BF16)
    return pl.pallas_call(
        conv_kernel(total, phases, n),
        out_shape=[
            jax.ShapeDtypeStruct((rows, 3 * middle), BF16),
            jax.ShapeDtypeStruct((rows, middle), F32),
            jax.ShapeDtypeStruct((2, middle), F32),
        ]
        + [slot] * n,
        scratch_shapes=[pltpu.VMEM((tiles, phases * middle), BF16)],
        compiler_params=params(),
        name="dilated_conv",
    )(sums, gain, bias, table, perm, weight, *slots)


def third_stats_kernel(total):
    def kernel(*refs):
        sums_ref, gain_ref, bias_ref, w_ref = refs[:4]
        slots = refs[4 : 4 + BLOCKS]
        act_ref, st_ref = refs[4 + BLOCKS :]
        mean, rs = moments(sums_ref[...], total)
        scale = gain_ref[...] * rs
        shift = bias_ref[...] - mean * scale
        acc = None
        for k in range(BLOCKS):
            u = slots[k][...].astype(F32) * scale + shift
            a = (u * sigmoid(u)).astype(BF16)
            act_ref[k] = a
            h = dot(a, w_ref[...])
            part = column_sums(h, h * h)
            acc = part if acc is None else acc + part
        st_ref[...] = acc

    return kernel


def third_stats_call(total, sums, gain, bias, weight, slots):
    rows, middle = slots[0].shape
    return pl.pallas_call(
        third_stats_kernel(total),
        out_shape=[
            jax.ShapeDtypeStruct((BLOCKS, rows, middle), BF16),
            jax.ShapeDtypeStruct((2, weight.shape[1]), F32),
        ],
        compiler_params=params(),
        name="third_stats",
    )(sums, gain, bias, weight, *slots)


def two_parts(value):
    high = value.astype(BF16)
    return high, (value - high.astype(F32)).astype(BF16)


def output_kernel(total):
    def kernel(me_ref, sums_ref, gain_ref, bias_ref, w_ref, a_ref, x_ref, ct_ref, y_ref, e_ref, low_ref, st_ref, *sends):
        step = pl.program_id(0)
        mean, rs = moments(sums_ref[...], total)
        h = dot(a_ref[0], w_ref[...])
        n = (h - mean) * rs
        z = gain_ref[...] * n + bias_ref[...] + x_ref[0].astype(F32)
        s = sigmoid(z)
        y = z * s
        y_ref[0] = y.astype(BF16)
        e = ct_ref[0].astype(F32) * (s + y * (1.0 - s))
        kept, low = two_parts(e * (gain_ref[...] * rs))
        e_ref[0] = kept
        low_ref[0] = low
        part = column_sums(e, e * n)

        @pl.when(step == 0)
        def _():
            st_ref[...] = part

        @pl.when(step > 0)
        def _():
            st_ref[...] += part

        raw = dot(kept, w_ref[...], ((1,), (1,))).astype(BF16)
        for k in range(BLOCKS):

            @pl.when(step == k)
            def _():
                sends[k][...] = raw

    return kernel


def output_call(total, me, sums, gain, bias, weight, act, inputs, cotangent):
    rows, middle = act.shape[1:]
    width = weight.shape[1]
    natural = pl.BlockSpec((1, rows, width), lambda b, me: (b ^ me[0], 0, 0))
    vector = pl.BlockSpec((1, width), lambda b, me: (0, 0))
    pair = pl.BlockSpec((2, width), lambda b, me: (0, 0))
    return pl.pallas_call(
        output_kernel(total),
        grid_spec=pltpu.PrefetchScalarGridSpec(
            num_scalar_prefetch=1,
            grid=(BLOCKS,),
            in_specs=[
                pair,
                vector,
                vector,
                pl.BlockSpec((middle, width), lambda b, me: (0, 0)),
                pl.BlockSpec((1, rows, middle), lambda b, me: (b, 0, 0)),
                natural,
                natural,
            ],
            out_specs=[natural, natural, natural, pair]
            + [pl.BlockSpec((rows, middle), lambda b, me: (0, 0))] * BLOCKS,
        ),
        out_shape=[jax.ShapeDtypeStruct((BLOCKS, rows, width), BF16)] * 3
        + [jax.ShapeDtypeStruct((2, width), F32)]
        + [jax.ShapeDtypeStruct((rows, middle), BF16)] * BLOCKS,
        compiler_params=params(1),
        name="block_output",
    )(me, sums, gain, bias, weight, act, inputs, cotangent)


def norm_coefficients(sums, grads, gain, total):
    mean, rs = moments(sums, total)
    keep = gain * rs
    slope = keep * rs * (grads[1:2] / total)
    offset = keep * (grads[0:1] / total) - slope * mean
    return keep, offset, slope


def third_grad_kernel(total):
    def kernel(me_ref, sums_ref, grads_ref, gain_ref, w_ref, a_ref, e_ref, low_ref, d_ref):
        _, offset, slope = norm_coefficients(sums_ref[...], grads_ref[...], gain_ref[...], total)
        h = dot(a_ref[0], w_ref[...])
        e = e_ref[0].astype(F32) + low_ref[0].astype(F32)
        d_ref[0] = (e - offset - slope * h).astype(BF16)

    return kernel


def third_grad_call(total, me, sums, grads, gain, weight, act, kept, low):
    rows, middle = act.shape[1:]
    width = weight.shape[1]
    vector = pl.BlockSpec((1, width), lambda b, me: (0, 0))
    pair = pl.BlockSpec((2, width), lambda b, me: (0, 0))
    slot = pl.BlockSpec((1, rows, width), lambda b, me: (b, 0, 0))
    return pl.pallas_call(
        third_grad_kernel(total),
        grid_spec=pltpu.PrefetchScalarGridSpec(
            num_scalar_prefetch=1,
            grid=(BLOCKS,),
            in_specs=[
                pair,
                pair,
                vector,
                pl.BlockSpec((middle, width), lambda b, me: (0, 0)),
                pl.BlockSpec((1, rows, middle), lambda b, me: (b, 0, 0)),
                pl.BlockSpec((1, rows, width), lambda b, me: (b ^ me[0], 0, 0)),
                pl.BlockSpec((1, rows, width), lambda b, me: (b ^ me[0], 0, 0)),
            ],
            out_specs=slot,
        ),
        out_shape=jax.ShapeDtypeStruct((BLOCKS, rows, width), BF16),
        compiler_params=params(1),
        name="third_grad",
    )(me, sums, grads, gain, weight, act, kept, low)


def correction_kernel(total):
    def kernel(sums3_ref, grads3_ref, gain3_ref, w_ref, sums2_ref, gain2_ref, bias2_ref, h_ref, o_ref):
        _, offset, slope = norm_coefficients(
            sums3_ref[...], grads3_ref[...], gain3_ref[...], total
        )
        w = w_ref[...]
        last = ((1,), (1,))
        high, low = two_parts(w.astype(F32) * slope)
        inner = dot(high, w, last) + dot(low, w, last)
        high, low = two_parts(inner)
        one, two = two_parts(jnp.broadcast_to(offset, (8, offset.shape[1])))
        three = (
            jnp.broadcast_to(offset, (8, offset.shape[1])) - one.astype(F32) - two.astype(F32)
        ).astype(BF16)
        constant = (dot(one, w, last) + dot(two, w, last) + dot(three, w, last))[0:1]
        mean, rs = moments(sums2_ref[...], total)
        scale = gain2_ref[...] * rs
        shift = bias2_ref[...] - mean * scale
        u = h_ref[...].astype(BF16).astype(F32) * scale + shift
        a = (u * sigmoid(u)).astype(BF16)
        o_ref[...] = constant + dot(a, high) + dot(a, low)

    return kernel


def correction_call(total, sums3, grads3, gain3, weight, sums2, gain2, bias2, hidden):
    return pl.pallas_call(
        correction_kernel(total),
        out_shape=jax.ShapeDtypeStruct(hidden.shape, F32),
        compiler_params=params(),
        name="third_grad_correction",
    )(sums3, grads3, gain3, weight, sums2, gain2, bias2, hidden)


def second_grad_kernel(total, phases, nslots):
    def kernel(*refs):
        sums_ref, gain_ref, bias_ref, tab_ref, perm_ref, h_ref, fix_ref = refs[:7]
        slots = refs[7 : 7 + nslots]
        e_ref, st_ref, wide_ref = refs[7 + nslots :]
        tiles = tab_ref.shape[0]
        each = tiles // nslots
        middle = h_ref.shape[1]
        for k in range(nslots):
            for j in range(phases):
                wide_ref[k * each : (k + 1) * each, j * middle : (j + 1) * middle] = slots[k][
                    j * each : (j + 1) * each, :
                ]
        da = dot(onehot(tab_ref[:, 1:2], perm_ref[...]), wide_ref[...])
        mean, rs = moments(sums_ref[...], total)
        acc = None
        for j in range(phases):
            n = (h_ref[j * tiles : (j + 1) * tiles, :] - mean) * rs
            u = gain_ref[...] * n + bias_ref[...]
            s = sigmoid(u)
            raw = da[:, j * middle : (j + 1) * middle] - fix_ref[j * tiles : (j + 1) * tiles, :]
            e = raw * (s * (1.0 + u * (1.0 - s)))
            e_ref[j * tiles : (j + 1) * tiles, :] = e
            part = column_sums(e, e * n)
            acc = part if acc is None else acc + part
        st_ref[...] = acc

    return kernel


def second_grad_call(total, phases, sums, gain, bias, table, perm, hidden, fix, slots):
    tiles = table.shape[0]
    rows, middle = hidden.shape
    return pl.pallas_call(
        second_grad_kernel(total, phases, len(slots)),
        out_shape=[
            jax.ShapeDtypeStruct((rows, middle), F32),
            jax.ShapeDtypeStruct((2, middle), F32),
        ],
        scratch_shapes=[pltpu.VMEM((tiles, phases * middle), BF16)],
        compiler_params=params(),
        name="second_grad",
    )(sums, gain, bias, table, perm, hidden, fix, *slots)


def conv_grad_kernel(total, phases, nslots):
    def kernel(*refs):
        sums_ref, grads_ref, gain_ref, tab_ref, h_ref, e_ref, w_ref = refs[:7]
        lefts_ref, d_ref, rights_ref = refs[7:10]
        sends = refs[10 : 10 + nslots]
        wide_ref, rows_ref = refs[10 + nslots :]
        tiles = tab_ref.shape[0]
        middle = h_ref.shape[1]
        rows = h_ref.shape[0]
        keep, offset, slope = norm_coefficients(sums_ref[...], grads_ref[...], gain_ref[...], total)
        left = side_mask(tab_ref, 3, phases)
        right = side_mask(tab_ref, 4, phases)
        d = keep * e_ref[...] - offset - slope * h_ref[...]
        packed = d.astype(BF16)
        d_ref[...] = packed
        lefts_ref[...] = (right * pltpu.roll(d, rows - 1, axis=0)).astype(BF16)
        rights_ref[...] = (left * pltpu.roll(d, 1, axis=0)).astype(BF16)
        for j in range(phases):
            wide_ref[:, j * middle : (j + 1) * middle] = packed[j * tiles : (j + 1) * tiles]
            rows_ref[j * tiles : (j + 1) * tiles, middle : 2 * middle] = packed[
                j * tiles : (j + 1) * tiles
            ]
        row = lax.broadcasted_iota(jnp.int32, (1, tiles), 1)
        for dy in (0, 2):
            picked = dot(onehot(tab_ref[:, dy : dy + 1], row), wide_ref[...]).astype(BF16)
            for j in range(phases):
                rows_ref[j * tiles : (j + 1) * tiles, dy * middle : (dy + 1) * middle] = picked[
                    :, j * middle : (j + 1) * middle
                ]
        parts = []
        for dx in range(3):
            part = None
            for dy in range(3):
                term = dot(
                    rows_ref[:, dy * middle : (dy + 1) * middle], w_ref[2 - dy, 2 - dx], ((1,), (1,))
                )
                part = term if part is None else part + term
            parts.append(part)
        da = shift_add(parts[1], parts[0], parts[2], left, right).astype(BF16)
        for j in range(phases):
            wide_ref[:, j * middle : (j + 1) * middle] = da[j * tiles : (j + 1) * tiles]
        scatter(tab_ref, wide_ref[...], sends, phases)

    return kernel


def conv_grad_call(total, phases, nslots, sums, grads, gain, table, hidden, e, weight):
    tiles = table.shape[0]
    rows, middle = hidden.shape
    slot = jax.ShapeDtypeStruct((rows // nslots, middle), BF16)
    return pl.pallas_call(
        conv_grad_kernel(total, phases, nslots),
        out_shape=[jax.ShapeDtypeStruct((rows, middle), BF16)] * 3 + [slot] * nslots,
        scratch_shapes=[
            pltpu.VMEM((tiles, phases * middle), BF16),
            pltpu.VMEM((rows, 3 * middle), BF16),
        ],
        compiler_params=params(),
        name="dilated_conv_grad",
    )(sums, grads, gain, table, hidden, e, weight)


def first_grad_kernel(total):
    def kernel(*refs):
        sums_ref, gain_ref, bias_ref = refs[:3]
        grads = refs[3 : 3 + BLOCKS]
        hiddens = refs[3 + BLOCKS : 3 + 2 * BLOCKS]
        e_ref, st_ref = refs[3 + 2 * BLOCKS :]
        mean, rs = moments(sums_ref[...], total)
        acc = None
        for k in range(BLOCKS):
            n = (hiddens[k][...].astype(F32) - mean) * rs
            u = gain_ref[...] * n + bias_ref[...]
            s = sigmoid(u)
            e = grads[k][...].astype(F32) * (s * (1.0 + u * (1.0 - s)))
            e_ref[k] = e
            part = column_sums(e, e * n)
            acc = part if acc is None else acc + part
        st_ref[...] = acc

    return kernel


def first_grad_call(total, sums, gain, bias, grads, hiddens):
    rows, middle = hiddens[0].shape
    return pl.pallas_call(
        first_grad_kernel(total),
        out_shape=[
            jax.ShapeDtypeStruct((BLOCKS, rows, middle), F32),
            jax.ShapeDtypeStruct((2, middle), F32),
        ],
        compiler_params=params(),
        name="first_grad",
    )(sums, gain, bias, *grads, *hiddens)


def first_hidden_grad_kernel(total):
    def kernel(me_ref, sums_ref, grads_ref, gain_ref, e_ref, *refs):
        hiddens = refs[:BLOCKS]
        d_ref = refs[BLOCKS]
        keep, offset, slope = norm_coefficients(sums_ref[...], grads_ref[...], gain_ref[...], total)
        for k in range(BLOCKS):
            d = keep * e_ref[k] - offset - slope * hiddens[k][...].astype(F32)
            d_ref[k ^ me_ref[0]] = d.astype(BF16)

    return kernel


def first_hidden_grad_call(total, me, sums, grads, gain, e, hiddens):
    rows, middle = hiddens[0].shape
    vmem = pl.BlockSpec(memory_space=pltpu.VMEM)
    return pl.pallas_call(
        first_hidden_grad_kernel(total),
        in_specs=[pl.BlockSpec(memory_space=pltpu.SMEM)] + [vmem] * (4 + BLOCKS),
        out_specs=vmem,
        out_shape=jax.ShapeDtypeStruct((BLOCKS, rows, middle), BF16),
        compiler_params=params(),
        name="first_hidden_grad",
    )(me, sums, grads, gain, e, *hiddens)


def input_grad_kernel(total):
    def kernel(sums_ref, gain_ref, d_ref, w_ref, e_ref, o_ref):
        _, rs = moments(sums_ref[...], total)
        undo = 1.0 / (gain_ref[...] * rs)
        o_ref[0] = dot(d_ref[0], w_ref[...], ((1,), (1,))) + e_ref[0].astype(F32) * undo

    return kernel


def input_grad_call(total, sums, gain, d, weight, kept):
    rows, middle = d.shape[1:]
    width = weight.shape[0]
    return pl.pallas_call(
        input_grad_kernel(total),
        grid=(BLOCKS,),
        in_specs=[
            pl.BlockSpec((2, width), lambda b: (0, 0)),
            pl.BlockSpec((1, width), lambda b: (0, 0)),
            pl.BlockSpec((1, rows, middle), lambda b: (b, 0, 0)),
            pl.BlockSpec((width, middle), lambda b: (0, 0)),
            pl.BlockSpec((1, rows, width), lambda b: (b, 0, 0)),
        ],
        out_specs=pl.BlockSpec((1, rows, width), lambda b: (b, 0, 0)),
        out_shape=jax.ShapeDtypeStruct((BLOCKS, rows, width), F32),
        compiler_params=params(1),
        name="input_grad",
    )(sums, gain, d, weight, kept)


def swap(value, mask, count):
    return lax.ppermute(value, AXES, [(i, i ^ mask) for i in range(count)])


def small_sum(value, count):
    if count != 32:
        return lax.psum(value, AXES)
    for masks in ((1,), (2, 4, 6), (8, 16, 24)):
        arrived = [value] + [swap(value, m, count) for m in masks]
        while len(arrived) > 1:
            arrived = [a + b for a, b in zip(arrived[::2], arrived[1::2])]
        value = arrived[0]
    return value


def by_bits(values, place, bits):
    for bit in range(bits):
        paired = values.reshape((1 << (bits - bit - 1), 2, 1 << bit) + values.shape[1:])
        flipped = paired[:, ::-1].reshape(values.shape)
        values = jnp.where(((place >> bit) & 1) == 1, flipped, values)
    return values


def scatter_sum(value, stages, index, count):
    for shift, bits in stages:
        n = 1 << bits
        mine = (index >> shift) & (n - 1)
        parts = value.reshape((n, value.shape[0] // n) + value.shape[1:])
        kept = lax.dynamic_index_in_dim(parts, mine, 0, keepdims=False).astype(F32)
        for m in range(1, n):
            leaving = lax.dynamic_index_in_dim(parts, mine ^ m, 0, keepdims=False)
            kept = kept + swap(leaving, m << shift, count).astype(F32)
        value = kept.astype(BF16)
    return value


def gather_back(value, stages, index, count):
    for shift, bits in stages[::-1]:
        n = 1 << bits
        arrived = [value] + [swap(value, m << shift, count) for m in range(1, n)]
        value = by_bits(jnp.stack(arrived), (index >> shift) & (n - 1), bits)
        value = value.reshape((n * value.shape[1],) + value.shape[2:])
    return value


STAGES = (((0, 1), (1, 1), (2, 1), (3, 2)), ((0, 1), (2, 1), (1, 1), (3, 2)))


def weight_sum(value, index, count):
    if count != 32:
        return lax.psum(value.astype(F32), AXES)
    halves = value.reshape((2, value.shape[0] // 2) + value.shape[1:])
    out = [
        gather_back(scatter_sum(halves[i], STAGES[i], index, count), STAGES[i], index, count)
        for i in range(2)
    ]
    return jnp.concatenate(out, axis=0).astype(F32)


SEND_ORDER = (6, 7, 4, 5, 2, 3, 1)


def exchange_slots(slots):
    out = [slots[0]] + [None] * (BLOCKS - 1)
    for k in SEND_ORDER:
        out[k] = lax.ppermute(slots[k], "dp", [(i, i ^ k) for i in range(BLOCKS)])
    return out


def body(
    block_in,
    crop_codes,
    tile_perm,
    reduce_weight,
    dilated_weight,
    expand_weight,
    first_gain,
    first_bias,
    middle_gain,
    middle_bias,
    last_gain,
    last_bias,
    cotangent,
):
    devices = lax.axis_size("dp")
    replicas = lax.axis_size("rep")
    count = devices * replicas
    sets = crop_codes.shape[1]
    phases = 16 * sets // devices
    pixels, width = block_in.shape[1:]
    middle = reduce_weight.shape[1]
    tiles = tile_perm.shape[2]
    each = tiles // devices
    rows = pixels // BLOCKS
    total = float(pixels * count)
    paired = devices == BLOCKS

    place = lax.axis_index("dp").astype(jnp.int32)
    me = (place if paired else jnp.zeros_like(place)).reshape(1)
    set_index = place * phases // 16
    codes = lax.dynamic_index_in_dim(crop_codes[0], set_index, 0, keepdims=False)
    order = lax.dynamic_index_in_dim(tile_perm[0], set_index, 0, keepdims=False)
    if paired:
        order = xor_blocks(order.reshape(BLOCKS, each), place).reshape(tiles)
    table = tile_table(codes, order, tiles)
    perm = order.reshape(1, tiles)

    def to_phases(slots):
        if paired:
            return exchange_slots(slots)
        joined = jnp.concatenate(slots, axis=0).reshape(devices, phases, each, middle)
        moved = lax.all_to_all(joined, "dp", split_axis=0, concat_axis=2, tiled=True)
        return [moved.reshape(phases * tiles, middle)]

    def to_pixels(slots):
        if paired:
            return exchange_slots(slots)
        parted = slots[0].reshape(phases, devices, each, middle)
        moved = lax.all_to_all(parted, "dp", split_axis=1, concat_axis=0, tiled=True)
        moved = moved.reshape(BLOCKS, rows, middle)
        return [moved[k] for k in range(BLOCKS)]

    flat = block_in[0]
    inputs = flat.reshape(BLOCKS, rows, width)
    upstream = cotangent[0].reshape(BLOCKS, rows, width)
    taps = dilated_weight.reshape(3, 3, middle, middle)
    gain1, bias1 = first_gain.reshape(1, middle), first_bias.reshape(1, middle)
    gain2, bias2 = middle_gain.reshape(1, middle), middle_bias.reshape(1, middle)
    gain3, bias3 = last_gain.reshape(1, width), last_bias.reshape(1, width)

    *hidden1, part = first_call(me, inputs, reduce_weight)
    slots = to_phases(hidden1)
    sums1 = small_sum(part, count)
    columns, hidden2, part, *slots = conv_call(
        total, phases, sums1, gain1, bias1, table, perm, taps, slots
    )
    nslots = len(slots)
    slots = to_pixels(slots)
    sums2 = small_sum(part, count)
    act2, part = third_stats_call(total, sums2, gain2, bias2, expand_weight, slots)
    sums3 = small_sum(part, count)
    block_out, kept, low, part, *slots = output_call(
        total, me, sums3, gain3, bias3, expand_weight, act2, inputs, upstream
    )
    slots = to_phases(slots)
    grads3 = small_sum(part, count)
    fix = correction_call(
        total, sums3, grads3, gain3, expand_weight, sums2, gain2, bias2, hidden2
    )
    grad3 = third_grad_call(total, me, sums3, grads3, gain3, expand_weight, act2, kept, low)
    expand_grad = dot(
        act2.reshape(pixels, middle), grad3.reshape(pixels, width), ((0,), (0,))
    )
    slots, expand_grad = lax.optimization_barrier((slots, expand_grad))
    e2, part = second_grad_call(
        total, phases, sums2, gain2, bias2, table, perm, hidden2, fix, slots
    )
    grads2 = small_sum(part, count)
    *shifted, = conv_grad_call(
        total, phases, nslots, sums2, grads2, gain2, table, hidden2, e2, taps
    )
    shifted, slots = shifted[:3], shifted[3:]
    slots = to_pixels(slots)
    dilated_grad = jnp.concatenate(
        [dot(columns, d, ((0,), (0,))).astype(BF16) for d in shifted], axis=0
    )
    e1, part = first_grad_call(total, sums1, gain1, bias1, slots, hidden1)
    grads1 = small_sum(part, count)
    grad1 = first_hidden_grad_call(total, me, sums1, grads1, gain1, e1, hidden1)
    reduce_grad = dot(flat, grad1.reshape(pixels, middle), ((0,), (0,))).astype(BF16)
    grad_in = input_grad_call(total, sums3, gain3, grad1, reduce_weight, kept)
    index = place * replicas + lax.axis_index("rep").astype(jnp.int32)
    expand_grad = lax.psum(expand_grad, AXES)
    dilated_grad = weight_sum(dilated_grad, index, count)
    dilated_grad = (
        dilated_grad.reshape(3, 3, middle, middle).transpose(1, 0, 2, 3).reshape(9 * middle, middle)
    )
    reduce_grad = weight_sum(reduce_grad, index, count)
    return (
        block_out.reshape(1, pixels, width),
        grad_in.reshape(1, pixels, width),
        reduce_grad,
        dilated_grad,
        expand_grad,
        grads1[1],
        grads1[0],
        grads2[1],
        grads2[0],
        grads3[1],
        grads3[0],
    )


def solution(mesh):
    in_specs = (
        P("rep", "dp", None),
        P("rep", None, None),
        P("rep", None, None),
        P(),
        P(),
        P(),
        P(),
        P(),
        P(),
        P(),
        P(),
        P(),
        P("rep", "dp", None),
    )
    out_specs = (P("rep", "dp", None),) * 2 + (P(),) * 9
    return jax.shard_map(body, mesh=mesh, in_specs=in_specs, out_specs=out_specs, check_vma=False)
```

```python
import jax
import jax.numpy as jnp
from jax import lax
from jax.experimental import pallas as pl
from jax.experimental.pallas import tpu as pltpu
from jax.sharding import PartitionSpec as P

EPS = 1e-05
F32 = jnp.float32
BF16 = jnp.bfloat16
VMEM_BYTES = 58 * 1024 * 1024
AXES = ("dp", "rep")


def params(grid_rank=0):
    kwargs = {"vmem_limit_bytes": VMEM_BYTES}
    if grid_rank:
        kwargs["dimension_semantics"] = ("arbitrary",) * grid_rank
    return pltpu.CompilerParams(**kwargs)


def sigmoid(v):
    return 0.5 * jnp.tanh(0.5 * v) + 0.5


def dot(a, b, dims=((1,), (0,))):
    return lax.dot_general(a, b, (dims, ((), ())), preferred_element_type=F32)


def moments(sums, total):
    mean = sums[0:1] / total
    scale = lax.rsqrt(sums[1:2] / total - mean * mean + EPS)
    return mean, scale


def column_sums(a, b):
    return jnp.concatenate(
        [jnp.sum(a, axis=0, keepdims=True), jnp.sum(b, axis=0, keepdims=True)], axis=0
    )


def tile_table(codes, order, tiles):
    slots = codes.shape[0]
    sizes = 8 * codes * codes
    before = jnp.arange(slots)[:, None] <= jnp.arange(slots)[None, :]
    ending = jnp.sum(jnp.where(before, sizes[:, None], 0), axis=0, dtype=jnp.int32)
    number = jnp.arange(tiles, dtype=jnp.int32)
    started = (ending - sizes)[None, :] <= number[:, None]
    mine = started & (number[:, None] < ending[None, :])
    first = jnp.sum(jnp.where(mine, (ending - sizes)[None, :], 0), axis=1, dtype=jnp.int32)
    scale = jnp.sum(jnp.where(mine, codes[None, :], 0), axis=1, dtype=jnp.int32)
    width = 4 * scale
    height = 2 * scale
    local = number - first
    across = local // width
    along = local - across * width
    above = jnp.where(across > 0, number - width, -1)
    below = jnp.where(across < height - 1, number + width, -1)
    left = (along > 0).astype(jnp.int32)
    right = (along < width - 1).astype(jnp.int32)
    zero = jnp.zeros_like(number)
    return jnp.stack([above, number, below, left, right, order, zero, zero], axis=1)


STEPS = 4
CHUNK = 512


def first_kernel(x_ref, w_ref, o_ref, st_ref):
    step = pl.program_id(0)
    h = dot(x_ref[...], w_ref[...])
    o_ref[...] = h.astype(BF16)
    part = column_sums(h, h * h)

    @pl.when(step == 0)
    def _():
        st_ref[...] = part

    @pl.when(step > 0)
    def _():
        st_ref[...] += part


def first_call(inputs, weight):
    pixels, width = inputs.shape
    middle = weight.shape[1]
    rows = pixels // STEPS
    return pl.pallas_call(
        first_kernel,
        grid=(STEPS,),
        in_specs=[
            pl.BlockSpec((rows, width), lambda b: (b, 0)),
            pl.BlockSpec((width, middle), lambda b: (0, 0)),
        ],
        out_specs=[
            pl.BlockSpec((rows, middle), lambda b: (b, 0)),
            pl.BlockSpec((2, middle), lambda b: (0, 0)),
        ],
        out_shape=[
            jax.ShapeDtypeStruct((pixels, middle), BF16),
            jax.ShapeDtypeStruct((2, middle), F32),
        ],
        compiler_params=params(1),
        name="first_matmul",
    )(inputs, weight)


def side_mask(tab_ref, column, phases):
    mask = tab_ref[:, column : column + 1].astype(F32)
    return jnp.concatenate([mask] * phases, axis=0) if phases > 1 else mask


def onehot(column, row):
    return jnp.where(column == row, 1.0, 0.0).astype(BF16)


def shift_add(center, left, right, left_mask, right_mask):
    rows = center.shape[0]
    return (
        center
        + left_mask * pltpu.roll(left, 1, axis=0)
        + right_mask * pltpu.roll(right, rows - 1, axis=0)
    )


def spread(slots_ref, wide_ref, phases, change=lambda v: v):
    n, rows, middle = slots_ref.shape
    each = rows // phases
    for k in range(n):
        for j in range(phases):
            wide_ref[k * each : (k + 1) * each, j * middle : (j + 1) * middle] = change(
                slots_ref[k, j * each : (j + 1) * each, :]
            )


def scatter(tab_ref, wide, sends_ref, phases):
    n, rows, middle = sends_ref.shape
    each = rows // phases
    row = lax.broadcasted_iota(jnp.int32, (1, n * each), 1)
    back = dot(onehot(tab_ref[:, 5:6], row), wide).astype(BF16)
    for k in range(n):
        for j in range(phases):
            sends_ref[k, j * each : (j + 1) * each, :] = back[
                k * each : (k + 1) * each, j * middle : (j + 1) * middle
            ]


def conv_kernel(total, phases):
    def kernel(
        sums_ref, gain_ref, bias_ref, tab_ref, perm_ref, w_ref, slots_ref,
        cols_ref, h_ref, st_ref, sends_ref, act_ref,
    ):
        tiles = tab_ref.shape[0]
        middle = h_ref.shape[1]
        mean, rs = moments(sums_ref[...], total)
        scale = gain_ref[...] * rs
        shift = bias_ref[...] - mean * scale

        def activate(v):
            u = v.astype(F32) * scale + shift
            return (u * sigmoid(u)).astype(BF16)

        spread(slots_ref, act_ref, phases, activate)
        row = perm_ref[...]
        for dy in range(3):
            picked = dot(onehot(tab_ref[:, dy : dy + 1], row), act_ref[...]).astype(BF16)
            for j in range(phases):
                cols_ref[j * tiles : (j + 1) * tiles, dy * middle : (dy + 1) * middle] = picked[
                    :, j * middle : (j + 1) * middle
                ]
        parts = [
            dot(cols_ref[...], w_ref[:, dx].reshape(3 * middle, middle)) for dx in range(3)
        ]
        h = shift_add(
            parts[1], parts[0], parts[2], side_mask(tab_ref, 3, phases), side_mask(tab_ref, 4, phases)
        )
        h_ref[...] = h
        st_ref[...] = column_sums(h, h * h)
        packed = h.astype(BF16)
        for j in range(phases):
            act_ref[:, j * middle : (j + 1) * middle] = packed[j * tiles : (j + 1) * tiles]
        scatter(tab_ref, act_ref[...], sends_ref, phases)

    return kernel


def conv_call(total, phases, sums, gain, bias, table, perm, weight, slots):
    tiles = table.shape[0]
    middle = weight.shape[-1]
    rows = phases * tiles
    return pl.pallas_call(
        conv_kernel(total, phases),
        out_shape=[
            jax.ShapeDtypeStruct((rows, 3 * middle), BF16),
            jax.ShapeDtypeStruct((rows, middle), F32),
            jax.ShapeDtypeStruct((2, middle), F32),
            jax.ShapeDtypeStruct(slots.shape, BF16),
        ],
        scratch_shapes=[pltpu.VMEM((tiles, phases * middle), BF16)],
        compiler_params=params(),
        name="dilated_conv",
    )(sums, gain, bias, table, perm, weight, slots)


def third_stats_kernel(total):
    def kernel(sums_ref, gain_ref, bias_ref, w_ref, h_ref, act_ref, st_ref):
        mean, rs = moments(sums_ref[...], total)
        scale = gain_ref[...] * rs
        shift = bias_ref[...] - mean * scale
        pixels = h_ref.shape[0]
        width = w_ref.shape[1]
        chunk = min(CHUNK, width)
        rows = pixels // 2
        acc = [None] * (width // chunk)
        for i in range(2):
            u = h_ref[i * rows : (i + 1) * rows].astype(F32) * scale + shift
            a = (u * sigmoid(u)).astype(BF16)
            act_ref[i * rows : (i + 1) * rows] = a
            for c in range(width // chunk):
                h = dot(a, w_ref[:, c * chunk : (c + 1) * chunk])
                sums = column_sums(h, h * h)
                acc[c] = sums if acc[c] is None else acc[c] + sums
        for c in range(width // chunk):
            st_ref[:, c * chunk : (c + 1) * chunk] = acc[c]

    return kernel


def third_stats_call(total, sums, gain, bias, weight, hidden):
    return pl.pallas_call(
        third_stats_kernel(total),
        out_shape=[
            jax.ShapeDtypeStruct(hidden.shape, BF16),
            jax.ShapeDtypeStruct((2, weight.shape[1]), F32),
        ],
        compiler_params=params(),
        name="third_stats",
    )(sums, gain, bias, weight, hidden)


def two_parts(value):
    high = value.astype(BF16)
    return high, (value - high.astype(F32)).astype(BF16)


def output_kernel(total):
    def kernel(
        sums_ref, gain_ref, bias_ref, w_ref, a_ref, x_ref, ct_ref,
        y_ref, e_ref, low_ref, st_ref, raw_ref,
    ):
        step = pl.program_id(0)
        a = a_ref[...]
        width = w_ref.shape[1]
        chunk = min(CHUNK, width)
        raw = None

        @pl.when(step == 0)
        def _():
            st_ref[...] = jnp.zeros_like(st_ref)

        for c in range(0, width, chunk):
            at = slice(c, c + chunk)
            mean, rs = moments(sums_ref[:, at], total)
            keep = gain_ref[:, at] * rs
            shift = bias_ref[:, at] - mean * keep
            w = w_ref[:, at]
            h = dot(a, w)
            z = keep * h + shift + x_ref[:, at].astype(F32)
            s = sigmoid(z)
            y = z * s
            y_ref[:, at] = y.astype(BF16)
            e = ct_ref[:, at].astype(F32) * (s + y * (1.0 - s))
            kept, low = two_parts(e * keep)
            e_ref[:, at] = kept
            low_ref[:, at] = low
            sums = column_sums(e, e * h)
            st_ref[0:1, at] += sums[0:1]
            st_ref[1:2, at] += (sums[1:2] - mean * sums[0:1]) * rs
            term = dot(kept, w, ((1,), (1,)))
            raw = term if raw is None else raw + term
        raw_ref[...] = raw.astype(BF16)

    return kernel


def output_call(total, sums, gain, bias, weight, act, inputs, cotangent):
    pixels, middle = act.shape
    width = weight.shape[1]
    rows = pixels // STEPS
    block = pl.BlockSpec((rows, width), lambda b: (b, 0))
    narrow = pl.BlockSpec((rows, middle), lambda b: (b, 0))
    vector = pl.BlockSpec((1, width), lambda b: (0, 0))
    pair = pl.BlockSpec((2, width), lambda b: (0, 0))
    return pl.pallas_call(
        output_kernel(total),
        grid=(STEPS,),
        in_specs=[
            pair,
            vector,
            vector,
            pl.BlockSpec((middle, width), lambda b: (0, 0)),
            narrow,
            block,
            block,
        ],
        out_specs=[block, block, block, pair, narrow],
        out_shape=[jax.ShapeDtypeStruct((pixels, width), BF16)] * 3
        + [
            jax.ShapeDtypeStruct((2, width), F32),
            jax.ShapeDtypeStruct((pixels, middle), BF16),
        ],
        compiler_params=params(1),
        name="block_output",
    )(sums, gain, bias, weight, act, inputs, cotangent)


def norm_coefficients(sums, grads, gain, total):
    mean, rs = moments(sums, total)
    keep = gain * rs
    slope = keep * rs * (grads[1:2] / total)
    offset = keep * (grads[0:1] / total) - slope * mean
    return keep, offset, slope


def third_grad_kernel(total):
    def kernel(sums_ref, grads_ref, gain_ref, w_ref, a_ref, e_ref, low_ref, d_ref):
        width = w_ref.shape[1]
        chunk = min(CHUNK, width)
        a = a_ref[...]
        for c in range(0, width, chunk):
            at = slice(c, c + chunk)
            _, offset, slope = norm_coefficients(
                sums_ref[:, at], grads_ref[:, at], gain_ref[:, at], total
            )
            h = dot(a, w_ref[:, at])
            e = e_ref[:, at].astype(F32) + low_ref[:, at].astype(F32)
            d_ref[:, at] = (e - offset - slope * h).astype(BF16)

    return kernel


def third_grad_call(total, sums, grads, gain, weight, act, kept, low):
    pixels, middle = act.shape
    width = weight.shape[1]
    rows = pixels // STEPS
    vector = pl.BlockSpec((1, width), lambda b: (0, 0))
    pair = pl.BlockSpec((2, width), lambda b: (0, 0))
    block = pl.BlockSpec((rows, width), lambda b: (b, 0))
    return pl.pallas_call(
        third_grad_kernel(total),
        grid=(STEPS,),
        in_specs=[
            pair,
            pair,
            vector,
            pl.BlockSpec((middle, width), lambda b: (0, 0)),
            pl.BlockSpec((rows, middle), lambda b: (b, 0)),
            block,
            block,
        ],
        out_specs=block,
        out_shape=jax.ShapeDtypeStruct((pixels, width), BF16),
        compiler_params=params(1),
        name="third_grad",
    )(sums, grads, gain, weight, act, kept, low)


def correction_kernel(total):
    def kernel(sums3_ref, grads3_ref, gain3_ref, w_ref, sums2_ref, gain2_ref, bias2_ref, h_ref, o_ref):
        _, offset, slope = norm_coefficients(
            sums3_ref[...], grads3_ref[...], gain3_ref[...], total
        )
        w = w_ref[...]
        last = ((1,), (1,))
        high, low = two_parts(w.astype(F32) * slope)
        inner = dot(high, w, last) + dot(low, w, last)
        high, low = two_parts(inner)
        one, two = two_parts(jnp.broadcast_to(offset, (8, offset.shape[1])))
        three = (
            jnp.broadcast_to(offset, (8, offset.shape[1])) - one.astype(F32) - two.astype(F32)
        ).astype(BF16)
        constant = (dot(one, w, last) + dot(two, w, last) + dot(three, w, last))[0:1]
        mean, rs = moments(sums2_ref[...], total)
        scale = gain2_ref[...] * rs
        shift = bias2_ref[...] - mean * scale
        u = h_ref[...].astype(BF16).astype(F32) * scale + shift
        a = (u * sigmoid(u)).astype(BF16)
        o_ref[...] = constant + dot(a, high) + dot(a, low)

    return kernel


def correction_call(total, sums3, grads3, gain3, weight, sums2, gain2, bias2, hidden):
    return pl.pallas_call(
        correction_kernel(total),
        out_shape=jax.ShapeDtypeStruct(hidden.shape, F32),
        compiler_params=params(),
        name="third_grad_correction",
    )(sums3, grads3, gain3, weight, sums2, gain2, bias2, hidden)


def second_grad_kernel(total, phases):
    def kernel(
        sums_ref, gain_ref, bias_ref, tab_ref, perm_ref, h_ref, fix_ref, slots_ref,
        e_ref, st_ref, wide_ref,
    ):
        tiles = tab_ref.shape[0]
        middle = h_ref.shape[1]
        spread(slots_ref, wide_ref, phases)
        da = dot(onehot(tab_ref[:, 1:2], perm_ref[...]), wide_ref[...])
        mean, rs = moments(sums_ref[...], total)
        acc = None
        for j in range(phases):
            at = slice(j * tiles, (j + 1) * tiles)
            n = (h_ref[at, :] - mean) * rs
            u = gain_ref[...] * n + bias_ref[...]
            s = sigmoid(u)
            e = (da[:, j * middle : (j + 1) * middle] - fix_ref[at, :]) * (s * (1.0 + u * (1.0 - s)))
            e_ref[at, :] = e
            part = column_sums(e, e * n)
            acc = part if acc is None else acc + part
        st_ref[...] = acc

    return kernel


def second_grad_call(total, phases, sums, gain, bias, table, perm, hidden, fix, slots):
    tiles = table.shape[0]
    rows, middle = hidden.shape
    return pl.pallas_call(
        second_grad_kernel(total, phases),
        out_shape=[
            jax.ShapeDtypeStruct((rows, middle), F32),
            jax.ShapeDtypeStruct((2, middle), F32),
        ],
        scratch_shapes=[pltpu.VMEM((tiles, phases * middle), BF16)],
        compiler_params=params(),
        name="second_grad",
    )(sums, gain, bias, table, perm, hidden, fix, slots)


def conv_grad_kernel(total, phases):
    def kernel(
        sums_ref, grads_ref, gain_ref, tab_ref, h_ref, e_ref, w_ref,
        lefts_ref, d_ref, rights_ref, sends_ref, wide_ref, rows_ref,
    ):
        tiles = tab_ref.shape[0]
        middle = h_ref.shape[1]
        rows = h_ref.shape[0]
        keep, offset, slope = norm_coefficients(sums_ref[...], grads_ref[...], gain_ref[...], total)
        left = side_mask(tab_ref, 3, phases)
        right = side_mask(tab_ref, 4, phases)
        d = keep * e_ref[...] - offset - slope * h_ref[...]
        packed = d.astype(BF16)
        d_ref[...] = packed
        lefts_ref[...] = (right * pltpu.roll(d, rows - 1, axis=0)).astype(BF16)
        rights_ref[...] = (left * pltpu.roll(d, 1, axis=0)).astype(BF16)
        for j in range(phases):
            wide_ref[:, j * middle : (j + 1) * middle] = packed[j * tiles : (j + 1) * tiles]
            rows_ref[j * tiles : (j + 1) * tiles, middle : 2 * middle] = packed[
                j * tiles : (j + 1) * tiles
            ]
        row = lax.broadcasted_iota(jnp.int32, (1, tiles), 1)
        for dy in (0, 2):
            picked = dot(onehot(tab_ref[:, dy : dy + 1], row), wide_ref[...]).astype(BF16)
            for j in range(phases):
                rows_ref[j * tiles : (j + 1) * tiles, dy * middle : (dy + 1) * middle] = picked[
                    :, j * middle : (j + 1) * middle
                ]
        parts = []
        for dx in range(3):
            part = None
            for dy in range(3):
                term = dot(
                    rows_ref[:, dy * middle : (dy + 1) * middle], w_ref[2 - dy, 2 - dx], ((1,), (1,))
                )
                part = term if part is None else part + term
            parts.append(part)
        da = shift_add(parts[1], parts[0], parts[2], left, right).astype(BF16)
        for j in range(phases):
            wide_ref[:, j * middle : (j + 1) * middle] = da[j * tiles : (j + 1) * tiles]
        scatter(tab_ref, wide_ref[...], sends_ref, phases)

    return kernel


def conv_grad_call(total, phases, sums, grads, gain, table, hidden, e, weight, shape):
    tiles = table.shape[0]
    rows, middle = hidden.shape
    return pl.pallas_call(
        conv_grad_kernel(total, phases),
        out_shape=[jax.ShapeDtypeStruct((rows, middle), BF16)] * 3
        + [jax.ShapeDtypeStruct(shape, BF16)],
        scratch_shapes=[
            pltpu.VMEM((tiles, phases * middle), BF16),
            pltpu.VMEM((rows, 3 * middle), BF16),
        ],
        compiler_params=params(),
        name="dilated_conv_grad",
    )(sums, grads, gain, table, hidden, e, weight)


def first_grad_kernel(total):
    def kernel(sums_ref, gain_ref, bias_ref, da_ref, h_ref, e_ref, st_ref):
        mean, rs = moments(sums_ref[...], total)
        n = (h_ref[...].astype(F32) - mean) * rs
        u = gain_ref[...] * n + bias_ref[...]
        s = sigmoid(u)
        e = da_ref[...].astype(F32) * (s * (1.0 + u * (1.0 - s)))
        e_ref[...] = e
        st_ref[...] = column_sums(e, e * n)

    return kernel


def first_grad_call(total, sums, gain, bias, grads, hidden):
    return pl.pallas_call(
        first_grad_kernel(total),
        out_shape=[
            jax.ShapeDtypeStruct(hidden.shape, F32),
            jax.ShapeDtypeStruct((2, hidden.shape[1]), F32),
        ],
        compiler_params=params(),
        name="first_grad",
    )(sums, gain, bias, grads, hidden)


def first_hidden_grad_kernel(total):
    def kernel(sums_ref, grads_ref, gain_ref, e_ref, h_ref, d_ref):
        keep, offset, slope = norm_coefficients(sums_ref[...], grads_ref[...], gain_ref[...], total)
        d_ref[...] = (keep * e_ref[...] - offset - slope * h_ref[...].astype(F32)).astype(BF16)

    return kernel


def first_hidden_grad_call(total, sums, grads, gain, e, hidden):
    return pl.pallas_call(
        first_hidden_grad_kernel(total),
        out_shape=jax.ShapeDtypeStruct(hidden.shape, BF16),
        compiler_params=params(),
        name="first_hidden_grad",
    )(sums, grads, gain, e, hidden)


def input_grad_kernel(total):
    def kernel(sums_ref, gain_ref, d_ref, w_ref, e_ref, *refs):
        o_ref = refs[-1]
        _, rs = moments(sums_ref[...], total)
        undo = 1.0 / (gain_ref[...] * rs)
        width = w_ref.shape[0]
        chunk = min(CHUNK, width)
        d = d_ref[...]
        for c in range(0, width, chunk):
            at = slice(c, c + chunk)
            o_ref[:, at] = (
                dot(d, w_ref[at, :], ((1,), (1,))) + e_ref[:, at].astype(F32) * undo[:, at]
            )

    return kernel


def input_grad_call(total, half, sums, gain, d, weight, kept, outs):
    pixels, middle = d.shape
    width = weight.shape[0]
    rows = pixels // STEPS

    def place(b):
        return (2 * half + b, 0)

    return pl.pallas_call(
        input_grad_kernel(total),
        grid=(2,),
        in_specs=[
            pl.BlockSpec((2, width), lambda b: (0, 0)),
            pl.BlockSpec((1, width), lambda b: (0, 0)),
            pl.BlockSpec((rows, middle), place),
            pl.BlockSpec((width, middle), lambda b: (0, 0)),
            pl.BlockSpec((rows, width), place),
        ]
        + [pl.BlockSpec(memory_space=pl.ANY)] * len(outs),
        out_specs=pl.BlockSpec((rows, width), place),
        out_shape=jax.ShapeDtypeStruct((pixels, width), F32),
        input_output_aliases={5: 0} if outs else {},
        compiler_params=params(1),
        name="input_grad",
    )(sums, gain, d, weight, kept, *outs)


def swap(value, mask, count):
    return lax.ppermute(value, AXES, [(i, i ^ mask) for i in range(count)])


ALONG_Z, ALONG_XY, CORES = (8, 16, 24), (2, 4, 6), (1,)


def small_step(value, masks, count):
    arrived = [value] + [swap(value, m, count) for m in masks]
    while len(arrived) > 1:
        arrived = [a + b for a, b in zip(arrived[::2], arrived[1::2])]
    return arrived[0]


def small_sum(value, count, order=(CORES, ALONG_XY, ALONG_Z)):
    if count != 32:
        return lax.psum(value, AXES)
    for masks in order:
        value = small_step(value, masks, count)
    return value


def by_bits(values, place, bits):
    for bit in range(bits):
        paired = values.reshape((1 << (bits - bit - 1), 2, 1 << bit) + values.shape[1:])
        flipped = paired[:, ::-1].reshape(values.shape)
        values = jnp.where(((place >> bit) & 1) == 1, flipped, values)
    return values


def scatter_step(value, stage, index, count):
    shift, bits = stage
    n = 1 << bits
    mine = (index >> shift) & (n - 1)
    parts = value.reshape((n, value.shape[0] // n) + value.shape[1:])
    kept = lax.dynamic_index_in_dim(parts, mine, 0, keepdims=False).astype(F32)
    for m in range(1, n):
        leaving = lax.dynamic_index_in_dim(parts, mine ^ m, 0, keepdims=False)
        kept = kept + swap(leaving, m << shift, count).astype(F32)
    return kept.astype(BF16)


def gather_step(value, stage, index, count):
    shift, bits = stage
    n = 1 << bits
    arrived = [value] + [swap(value, m << shift, count) for m in range(1, n)]
    value = by_bits(jnp.stack(arrived), (index >> shift) & (n - 1), bits)
    return value.reshape((n * value.shape[1],) + value.shape[2:])


STAGES = (((0, 1), (1, 1), (2, 1), (3, 2)), ((0, 1), (2, 1), (1, 1), (3, 2)))


def scatter_steps(halves, step, index, count):
    return [scatter_step(halves[i], STAGES[i][step], index, count) for i in range(2)]


def gather_steps(halves, step, index, count):
    return [gather_step(halves[i], STAGES[i][step], index, count) for i in range(2)]


def body(
    block_in,
    crop_codes,
    tile_perm,
    reduce_weight,
    dilated_weight,
    expand_weight,
    first_gain,
    first_bias,
    middle_gain,
    middle_bias,
    last_gain,
    last_bias,
    cotangent,
):
    devices = lax.axis_size("dp")
    replicas = lax.axis_size("rep")
    count = devices * replicas
    sets = crop_codes.shape[1]
    phases = 16 * sets // devices
    pixels, width = block_in.shape[1:]
    middle = reduce_weight.shape[1]
    tiles = tile_perm.shape[2]
    each = tiles // devices
    total = float(pixels * count)

    place = lax.axis_index("dp").astype(jnp.int32)
    set_index = place * phases // 16
    codes = lax.dynamic_index_in_dim(crop_codes[0], set_index, 0, keepdims=False)
    order = lax.dynamic_index_in_dim(tile_perm[0], set_index, 0, keepdims=False)
    table = tile_table(codes, order, tiles)
    perm = order.reshape(1, tiles)
    parted = (devices, phases * each, middle) if phases > 1 else (1, tiles, middle)

    def exchange(values):
        values = values.reshape(devices, phases * each, middle)
        return lax.all_to_all(values, "dp", split_axis=0, concat_axis=0, tiled=True)

    def to_phases(values):
        return exchange(values).reshape(parted)

    def to_pixels(values):
        return exchange(values).reshape(pixels, middle)

    flat = block_in[0]
    upstream = cotangent[0]
    taps = dilated_weight.reshape(3, 3, middle, middle)
    gain1, bias1 = first_gain.reshape(1, middle), first_bias.reshape(1, middle)
    gain2, bias2 = middle_gain.reshape(1, middle), middle_bias.reshape(1, middle)
    gain3, bias3 = last_gain.reshape(1, width), last_bias.reshape(1, width)

    index = place * replicas + lax.axis_index("rep").astype(jnp.int32)
    tree = count == 32

    def after(value, other):
        return lax.optimization_barrier((value, other)) if tree else (value, other)

    def halves_of(value):
        return [value[: value.shape[0] // 2], value[value.shape[0] // 2 :]]

    def scatter(value, step):
        return scatter_steps(value, step, index, count) if tree else value

    hidden1, part = first_call(flat, reduce_weight)
    slots = to_phases(hidden1)
    sums1 = small_sum(part, count)
    columns, hidden2, part, slots = conv_call(
        total, phases, sums1, gain1, bias1, table, perm, taps, slots
    )
    arrived = to_pixels(slots)
    sums2 = small_sum(part, count)
    act2, part = third_stats_call(total, sums2, gain2, bias2, expand_weight, arrived)
    sums3 = small_sum(part, count)
    block_out, kept, low, part, raw = output_call(
        total, sums3, gain3, bias3, expand_weight, act2, flat, upstream
    )
    if tree:
        part = small_step(part, ALONG_Z, count)
        raw, part = after(raw, part)
    slots = to_phases(raw)
    grads3 = small_sum(part, count, (ALONG_XY, CORES))
    fix = correction_call(
        total, sums3, grads3, gain3, expand_weight, sums2, gain2, bias2, hidden2
    )
    grad3 = third_grad_call(total, sums3, grads3, gain3, expand_weight, act2, kept, low)
    expand_grad = dot(act2, grad3, ((0,), (0,)))
    slots, expand_grad = lax.optimization_barrier((slots, expand_grad))
    e2, part = second_grad_call(
        total, phases, sums2, gain2, bias2, table, perm, hidden2, fix, slots
    )
    grads2 = small_sum(part, count)
    *shifted, slots = conv_grad_call(
        total, phases, sums2, grads2, gain2, table, hidden2, e2, taps, parted
    )
    arrived = to_pixels(slots)
    dilated = halves_of(
        jnp.concatenate(
            [
                dot(columns[:, dy * middle : (dy + 1) * middle], d, ((0,), (0,))).astype(BF16)
                for dy in range(3)
                for d in shifted
            ],
            axis=0,
        )
    )
    arrived, dilated = after(arrived, dilated)
    e1, part = first_grad_call(total, sums1, gain1, bias1, arrived, hidden1)
    dilated = scatter(dilated, 0)
    grads1 = small_sum(part, count)
    grads1, dilated = after(grads1, dilated)
    grad1 = first_hidden_grad_call(total, sums1, grads1, gain1, e1, hidden1)
    dilated = scatter(dilated, 1)
    reduced = halves_of(dot(flat, grad1, ((0,), (0,))).astype(BF16))
    reduced = scatter(reduced, 0)
    grad1, dilated = after(grad1, dilated)
    grad_in = input_grad_call(total, 0, sums3, gain3, grad1, reduce_weight, kept, [])
    dilated = scatter(dilated, 2)
    (grad1, grad_in), (dilated, reduced) = after((grad1, grad_in), (dilated, reduced))
    grad_in = input_grad_call(total, 1, sums3, gain3, grad1, reduce_weight, kept, [grad_in])
    dilated = scatter(dilated, 3)
    reduced = scatter(reduced, 1)
    reduced, grad_in = after(reduced, grad_in)
    for step in (2, 3):
        reduced = scatter(reduced, step)
    expand_grad = lax.psum(expand_grad, AXES)
    if tree:
        for step in (3, 2, 1, 0):
            dilated = gather_steps(dilated, step, index, count)
            if step == 1:
                dilated, expand_grad = after(dilated, expand_grad)
            reduced = gather_steps(reduced, step, index, count)
    dilated_grad = jnp.concatenate(dilated, axis=0).astype(F32)
    reduce_grad = jnp.concatenate(reduced, axis=0).astype(F32)
    if not tree:
        dilated_grad, reduce_grad = lax.psum((dilated_grad, reduce_grad), AXES)
    return (
        block_out.reshape(1, pixels, width),
        grad_in.reshape(1, pixels, width),
        reduce_grad,
        dilated_grad,
        expand_grad,
        grads1[1],
        grads1[0],
        grads2[1],
        grads2[0],
        grads3[1],
        grads3[0],
    )


def solution(mesh):
    in_specs = (
        P("rep", "dp", None),
        P("rep", None, None),
        P("rep", None, None),
        P(),
        P(),
        P(),
        P(),
        P(),
        P(),
        P(),
        P(),
        P(),
        P("rep", "dp", None),
    )
    out_specs = (P("rep", "dp", None),) * 2 + (P(),) * 9
    return jax.shard_map(body, mesh=mesh, in_specs=in_specs, out_specs=out_specs, check_vma=False)
```

```python
import jax
import jax.numpy as jnp
from jax import lax
from jax.experimental import pallas as pl
from jax.experimental.pallas import tpu as pltpu
from jax.sharding import PartitionSpec as P

EPS = 1e-05
F32 = jnp.float32
BF16 = jnp.bfloat16
VMEM_BYTES = 58 * 1024 * 1024
AXES = ("dp", "rep")


def params(grid_rank=0):
    kwargs = {"vmem_limit_bytes": VMEM_BYTES}
    if grid_rank:
        kwargs["dimension_semantics"] = ("arbitrary",) * grid_rank
    return pltpu.CompilerParams(**kwargs)


def sigmoid(v):
    return 0.5 * jnp.tanh(0.5 * v) + 0.5


def dot(a, b, dims=((1,), (0,))):
    return lax.dot_general(a, b, (dims, ((), ())), preferred_element_type=F32)


def moments(sums, total):
    mean = sums[0:1] / total
    scale = lax.rsqrt(sums[1:2] / total - mean * mean + EPS)
    return mean, scale


def column_sums(a, b):
    return jnp.concatenate(
        [jnp.sum(a, axis=0, keepdims=True), jnp.sum(b, axis=0, keepdims=True)], axis=0
    )


def tile_table(codes, order, tiles):
    slots = codes.shape[0]
    sizes = 8 * codes * codes
    before = jnp.arange(slots)[:, None] <= jnp.arange(slots)[None, :]
    ending = jnp.sum(jnp.where(before, sizes[:, None], 0), axis=0, dtype=jnp.int32)
    number = jnp.arange(tiles, dtype=jnp.int32)
    started = (ending - sizes)[None, :] <= number[:, None]
    mine = started & (number[:, None] < ending[None, :])
    first = jnp.sum(jnp.where(mine, (ending - sizes)[None, :], 0), axis=1, dtype=jnp.int32)
    scale = jnp.sum(jnp.where(mine, codes[None, :], 0), axis=1, dtype=jnp.int32)
    width = 4 * scale
    height = 2 * scale
    local = number - first
    across = local // width
    along = local - across * width
    above = jnp.where(across > 0, number - width, -1)
    below = jnp.where(across < height - 1, number + width, -1)
    left = (along > 0).astype(jnp.int32)
    right = (along < width - 1).astype(jnp.int32)
    zero = jnp.zeros_like(number)
    return jnp.stack([above, number, below, left, right, order, zero, zero], axis=1)


STEPS = 4
CHUNK = 512


def first_kernel(x_ref, w_ref, o_ref, st_ref):
    step = pl.program_id(0)
    h = dot(x_ref[...], w_ref[...])
    o_ref[...] = h.astype(BF16)
    part = column_sums(h, h * h)

    @pl.when(step == 0)
    def _():
        st_ref[...] = part

    @pl.when(step > 0)
    def _():
        st_ref[...] += part


def first_call(inputs, weight):
    pixels, width = inputs.shape
    middle = weight.shape[1]
    rows = pixels // STEPS
    return pl.pallas_call(
        first_kernel,
        grid=(STEPS,),
        in_specs=[
            pl.BlockSpec((rows, width), lambda b: (b, 0)),
            pl.BlockSpec((width, middle), lambda b: (0, 0)),
        ],
        out_specs=[
            pl.BlockSpec((rows, middle), lambda b: (b, 0)),
            pl.BlockSpec((2, middle), lambda b: (0, 0)),
        ],
        out_shape=[
            jax.ShapeDtypeStruct((pixels, middle), BF16),
            jax.ShapeDtypeStruct((2, middle), F32),
        ],
        compiler_params=params(1),
        name="first_matmul",
    )(inputs, weight)


def side_mask(tab_ref, column, phases):
    mask = tab_ref[:, column : column + 1].astype(F32)
    return jnp.concatenate([mask] * phases, axis=0) if phases > 1 else mask


def onehot(column, row):
    return jnp.where(column == row, 1.0, 0.0).astype(BF16)


def shift_add(center, left, right, left_mask, right_mask):
    rows = center.shape[0]
    return (
        center
        + left_mask * pltpu.roll(left, 1, axis=0)
        + right_mask * pltpu.roll(right, rows - 1, axis=0)
    )


def spread(slots_ref, wide_ref, phases, change=lambda v: v):
    n, rows, middle = slots_ref.shape
    each = rows // phases
    for k in range(n):
        for j in range(phases):
            wide_ref[k * each : (k + 1) * each, j * middle : (j + 1) * middle] = change(
                slots_ref[k, j * each : (j + 1) * each, :]
            )


def scatter(tab_ref, wide, sends_ref, phases):
    n, rows, middle = sends_ref.shape
    each = rows // phases
    row = lax.broadcasted_iota(jnp.int32, (1, n * each), 1)
    back = dot(onehot(tab_ref[:, 5:6], row), wide).astype(BF16)
    for k in range(n):
        for j in range(phases):
            sends_ref[k, j * each : (j + 1) * each, :] = back[
                k * each : (k + 1) * each, j * middle : (j + 1) * middle
            ]


def conv_kernel(total, phases):
    def kernel(
        sums_ref, gain_ref, bias_ref, tab_ref, perm_ref, w_ref, slots_ref,
        cols_ref, h_ref, st_ref, sends_ref, act_ref,
    ):
        tiles = tab_ref.shape[0]
        middle = h_ref.shape[1]
        mean, rs = moments(sums_ref[...], total)
        scale = gain_ref[...] * rs
        shift = bias_ref[...] - mean * scale

        def activate(v):
            u = v.astype(F32) * scale + shift
            return (u * sigmoid(u)).astype(BF16)

        spread(slots_ref, act_ref, phases, activate)
        row = perm_ref[...]
        for dy in range(3):
            picked = dot(onehot(tab_ref[:, dy : dy + 1], row), act_ref[...]).astype(BF16)
            for j in range(phases):
                cols_ref[j * tiles : (j + 1) * tiles, dy * middle : (dy + 1) * middle] = picked[
                    :, j * middle : (j + 1) * middle
                ]
        parts = [
            dot(cols_ref[...], w_ref[:, dx].reshape(3 * middle, middle)) for dx in range(3)
        ]
        h = shift_add(
            parts[1], parts[0], parts[2], side_mask(tab_ref, 3, phases), side_mask(tab_ref, 4, phases)
        )
        h_ref[...] = h
        st_ref[...] = column_sums(h, h * h)
        packed = h.astype(BF16)
        for j in range(phases):
            act_ref[:, j * middle : (j + 1) * middle] = packed[j * tiles : (j + 1) * tiles]
        scatter(tab_ref, act_ref[...], sends_ref, phases)

    return kernel


def conv_call(total, phases, sums, gain, bias, table, perm, weight, slots):
    tiles = table.shape[0]
    middle = weight.shape[-1]
    rows = phases * tiles
    return pl.pallas_call(
        conv_kernel(total, phases),
        out_shape=[
            jax.ShapeDtypeStruct((rows, 3 * middle), BF16),
            jax.ShapeDtypeStruct((rows, middle), F32),
            jax.ShapeDtypeStruct((2, middle), F32),
            jax.ShapeDtypeStruct(slots.shape, BF16),
        ],
        scratch_shapes=[pltpu.VMEM((tiles, phases * middle), BF16)],
        compiler_params=params(),
        name="dilated_conv",
    )(sums, gain, bias, table, perm, weight, slots)


def third_stats_kernel(total):
    def kernel(sums_ref, gain_ref, bias_ref, w_ref, h_ref, act_ref, st_ref):
        mean, rs = moments(sums_ref[...], total)
        scale = gain_ref[...] * rs
        shift = bias_ref[...] - mean * scale
        pixels = h_ref.shape[0]
        width = w_ref.shape[1]
        chunk = min(CHUNK, width)
        rows = pixels // 2
        acc = [None] * (width // chunk)
        for i in range(2):
            u = h_ref[i * rows : (i + 1) * rows].astype(F32) * scale + shift
            a = (u * sigmoid(u)).astype(BF16)
            act_ref[i * rows : (i + 1) * rows] = a
            for c in range(width // chunk):
                h = dot(a, w_ref[:, c * chunk : (c + 1) * chunk])
                sums = column_sums(h, h * h)
                acc[c] = sums if acc[c] is None else acc[c] + sums
        for c in range(width // chunk):
            st_ref[:, c * chunk : (c + 1) * chunk] = acc[c]

    return kernel


def third_stats_call(total, sums, gain, bias, weight, hidden):
    return pl.pallas_call(
        third_stats_kernel(total),
        out_shape=[
            jax.ShapeDtypeStruct(hidden.shape, BF16),
            jax.ShapeDtypeStruct((2, weight.shape[1]), F32),
        ],
        compiler_params=params(),
        name="third_stats",
    )(sums, gain, bias, weight, hidden)


def two_parts(value):
    high = value.astype(BF16)
    return high, (value - high.astype(F32)).astype(BF16)


def output_kernel(total):
    def kernel(
        sums_ref, gain_ref, bias_ref, w_ref, a_ref, x_ref, ct_ref,
        y_ref, e_ref, low_ref, st_ref, raw_ref,
    ):
        step = pl.program_id(0)
        a = a_ref[...]
        width = w_ref.shape[1]
        chunk = min(CHUNK, width)
        raw = None

        @pl.when(step == 0)
        def _():
            st_ref[...] = jnp.zeros_like(st_ref)

        for c in range(0, width, chunk):
            at = slice(c, c + chunk)
            mean, rs = moments(sums_ref[:, at], total)
            keep = gain_ref[:, at] * rs
            shift = bias_ref[:, at] - mean * keep
            w = w_ref[:, at]
            h = dot(a, w)
            z = keep * h + shift + x_ref[:, at].astype(F32)
            s = sigmoid(z)
            y = z * s
            y_ref[:, at] = y.astype(BF16)
            e = ct_ref[:, at].astype(F32) * (s + y * (1.0 - s))
            kept, low = two_parts(e * keep)
            e_ref[:, at] = kept
            low_ref[:, at] = low
            sums = column_sums(e, e * h)
            st_ref[0:1, at] += sums[0:1]
            st_ref[1:2, at] += (sums[1:2] - mean * sums[0:1]) * rs
            term = dot(kept, w, ((1,), (1,)))
            raw = term if raw is None else raw + term
        raw_ref[...] = raw.astype(BF16)

    return kernel


def output_call(total, sums, gain, bias, weight, act, inputs, cotangent):
    pixels, middle = act.shape
    width = weight.shape[1]
    rows = pixels // STEPS
    block = pl.BlockSpec((rows, width), lambda b: (b, 0))
    narrow = pl.BlockSpec((rows, middle), lambda b: (b, 0))
    vector = pl.BlockSpec((1, width), lambda b: (0, 0))
    pair = pl.BlockSpec((2, width), lambda b: (0, 0))
    return pl.pallas_call(
        output_kernel(total),
        grid=(STEPS,),
        in_specs=[
            pair,
            vector,
            vector,
            pl.BlockSpec((middle, width), lambda b: (0, 0)),
            narrow,
            block,
            block,
        ],
        out_specs=[block, block, block, pair, narrow],
        out_shape=[jax.ShapeDtypeStruct((pixels, width), BF16)] * 3
        + [
            jax.ShapeDtypeStruct((2, width), F32),
            jax.ShapeDtypeStruct((pixels, middle), BF16),
        ],
        compiler_params=params(1),
        name="block_output",
    )(sums, gain, bias, weight, act, inputs, cotangent)


def norm_coefficients(sums, grads, gain, total):
    mean, rs = moments(sums, total)
    keep = gain * rs
    slope = keep * rs * (grads[1:2] / total)
    offset = keep * (grads[0:1] / total) - slope * mean
    return keep, offset, slope


def third_grad_kernel(total):
    def kernel(sums_ref, grads_ref, gain_ref, w_ref, a_ref, e_ref, low_ref, d_ref):
        width = w_ref.shape[1]
        chunk = min(CHUNK, width)
        a = a_ref[...]
        for c in range(0, width, chunk):
            at = slice(c, c + chunk)
            _, offset, slope = norm_coefficients(
                sums_ref[:, at], grads_ref[:, at], gain_ref[:, at], total
            )
            h = dot(a, w_ref[:, at])
            e = e_ref[:, at].astype(F32) + low_ref[:, at].astype(F32)
            d_ref[:, at] = (e - offset - slope * h).astype(BF16)

    return kernel


def third_grad_call(total, sums, grads, gain, weight, act, kept, low):
    pixels, middle = act.shape
    width = weight.shape[1]
    rows = pixels // STEPS
    vector = pl.BlockSpec((1, width), lambda b: (0, 0))
    pair = pl.BlockSpec((2, width), lambda b: (0, 0))
    block = pl.BlockSpec((rows, width), lambda b: (b, 0))
    return pl.pallas_call(
        third_grad_kernel(total),
        grid=(STEPS,),
        in_specs=[
            pair,
            pair,
            vector,
            pl.BlockSpec((middle, width), lambda b: (0, 0)),
            pl.BlockSpec((rows, middle), lambda b: (b, 0)),
            block,
            block,
        ],
        out_specs=block,
        out_shape=jax.ShapeDtypeStruct((pixels, width), BF16),
        compiler_params=params(1),
        name="third_grad",
    )(sums, grads, gain, weight, act, kept, low)


def correction_kernel(total):
    def kernel(sums3_ref, grads3_ref, gain3_ref, w_ref, sums2_ref, gain2_ref, bias2_ref, h_ref, o_ref):
        _, offset, slope = norm_coefficients(
            sums3_ref[...], grads3_ref[...], gain3_ref[...], total
        )
        w = w_ref[...]
        last = ((1,), (1,))
        high, low = two_parts(w.astype(F32) * slope)
        inner = dot(high, w, last) + dot(low, w, last)
        high, low = two_parts(inner)
        one, two = two_parts(jnp.broadcast_to(offset, (8, offset.shape[1])))
        three = (
            jnp.broadcast_to(offset, (8, offset.shape[1])) - one.astype(F32) - two.astype(F32)
        ).astype(BF16)
        constant = (dot(one, w, last) + dot(two, w, last) + dot(three, w, last))[0:1]
        mean, rs = moments(sums2_ref[...], total)
        scale = gain2_ref[...] * rs
        shift = bias2_ref[...] - mean * scale
        u = h_ref[...].astype(BF16).astype(F32) * scale + shift
        a = (u * sigmoid(u)).astype(BF16)
        o_ref[...] = constant + dot(a, high) + dot(a, low)

    return kernel


def correction_call(total, sums3, grads3, gain3, weight, sums2, gain2, bias2, hidden):
    return pl.pallas_call(
        correction_kernel(total),
        out_shape=jax.ShapeDtypeStruct(hidden.shape, F32),
        compiler_params=params(),
        name="third_grad_correction",
    )(sums3, grads3, gain3, weight, sums2, gain2, bias2, hidden)


def second_grad_kernel(total, phases):
    def kernel(
        sums_ref, gain_ref, bias_ref, tab_ref, perm_ref, h_ref, fix_ref, slots_ref,
        e_ref, st_ref, wide_ref,
    ):
        tiles = tab_ref.shape[0]
        middle = h_ref.shape[1]
        spread(slots_ref, wide_ref, phases)
        da = dot(onehot(tab_ref[:, 1:2], perm_ref[...]), wide_ref[...])
        mean, rs = moments(sums_ref[...], total)
        acc = None
        for j in range(phases):
            at = slice(j * tiles, (j + 1) * tiles)
            n = (h_ref[at, :] - mean) * rs
            u = gain_ref[...] * n + bias_ref[...]
            s = sigmoid(u)
            e = (da[:, j * middle : (j + 1) * middle] - fix_ref[at, :]) * (s * (1.0 + u * (1.0 - s)))
            e_ref[at, :] = e
            part = column_sums(e, e * n)
            acc = part if acc is None else acc + part
        st_ref[...] = acc

    return kernel


def second_grad_call(total, phases, sums, gain, bias, table, perm, hidden, fix, slots):
    tiles = table.shape[0]
    rows, middle = hidden.shape
    return pl.pallas_call(
        second_grad_kernel(total, phases),
        out_shape=[
            jax.ShapeDtypeStruct((rows, middle), F32),
            jax.ShapeDtypeStruct((2, middle), F32),
        ],
        scratch_shapes=[pltpu.VMEM((tiles, phases * middle), BF16)],
        compiler_params=params(),
        name="second_grad",
    )(sums, gain, bias, table, perm, hidden, fix, slots)


def conv_grad_kernel(total, phases):
    def kernel(
        sums_ref, grads_ref, gain_ref, tab_ref, h_ref, e_ref, w_ref,
        lefts_ref, d_ref, rights_ref, sends_ref, wide_ref, rows_ref,
    ):
        tiles = tab_ref.shape[0]
        middle = h_ref.shape[1]
        rows = h_ref.shape[0]
        keep, offset, slope = norm_coefficients(sums_ref[...], grads_ref[...], gain_ref[...], total)
        left = side_mask(tab_ref, 3, phases)
        right = side_mask(tab_ref, 4, phases)
        d = keep * e_ref[...] - offset - slope * h_ref[...]
        packed = d.astype(BF16)
        d_ref[...] = packed
        lefts_ref[...] = (right * pltpu.roll(d, rows - 1, axis=0)).astype(BF16)
        rights_ref[...] = (left * pltpu.roll(d, 1, axis=0)).astype(BF16)
        for j in range(phases):
            wide_ref[:, j * middle : (j + 1) * middle] = packed[j * tiles : (j + 1) * tiles]
            rows_ref[j * tiles : (j + 1) * tiles, middle : 2 * middle] = packed[
                j * tiles : (j + 1) * tiles
            ]
        row = lax.broadcasted_iota(jnp.int32, (1, tiles), 1)
        for dy in (0, 2):
            picked = dot(onehot(tab_ref[:, dy : dy + 1], row), wide_ref[...]).astype(BF16)
            for j in range(phases):
                rows_ref[j * tiles : (j + 1) * tiles, dy * middle : (dy + 1) * middle] = picked[
                    :, j * middle : (j + 1) * middle
                ]
        parts = []
        for dx in range(3):
            part = None
            for dy in range(3):
                term = dot(
                    rows_ref[:, dy * middle : (dy + 1) * middle], w_ref[2 - dy, 2 - dx], ((1,), (1,))
                )
                part = term if part is None else part + term
            parts.append(part)
        da = shift_add(parts[1], parts[0], parts[2], left, right).astype(BF16)
        for j in range(phases):
            wide_ref[:, j * middle : (j + 1) * middle] = da[j * tiles : (j + 1) * tiles]
        scatter(tab_ref, wide_ref[...], sends_ref, phases)

    return kernel


def conv_grad_call(total, phases, sums, grads, gain, table, hidden, e, weight, shape):
    tiles = table.shape[0]
    rows, middle = hidden.shape
    return pl.pallas_call(
        conv_grad_kernel(total, phases),
        out_shape=[jax.ShapeDtypeStruct((rows, middle), BF16)] * 3
        + [jax.ShapeDtypeStruct(shape, BF16)],
        scratch_shapes=[
            pltpu.VMEM((tiles, phases * middle), BF16),
            pltpu.VMEM((rows, 3 * middle), BF16),
        ],
        compiler_params=params(),
        name="dilated_conv_grad",
    )(sums, grads, gain, table, hidden, e, weight)


def first_grad_kernel(total):
    def kernel(sums_ref, gain_ref, bias_ref, da_ref, h_ref, e_ref, st_ref):
        mean, rs = moments(sums_ref[...], total)
        n = (h_ref[...].astype(F32) - mean) * rs
        u = gain_ref[...] * n + bias_ref[...]
        s = sigmoid(u)
        e = da_ref[...].astype(F32) * (s * (1.0 + u * (1.0 - s)))
        e_ref[...] = e
        st_ref[...] = column_sums(e, e * n)

    return kernel


def first_grad_call(total, sums, gain, bias, grads, hidden):
    return pl.pallas_call(
        first_grad_kernel(total),
        out_shape=[
            jax.ShapeDtypeStruct(hidden.shape, F32),
            jax.ShapeDtypeStruct((2, hidden.shape[1]), F32),
        ],
        compiler_params=params(),
        name="first_grad",
    )(sums, gain, bias, grads, hidden)


def first_hidden_grad_kernel(total):
    def kernel(sums_ref, grads_ref, gain_ref, e_ref, h_ref, d_ref):
        keep, offset, slope = norm_coefficients(sums_ref[...], grads_ref[...], gain_ref[...], total)
        d_ref[...] = (keep * e_ref[...] - offset - slope * h_ref[...].astype(F32)).astype(BF16)

    return kernel


def first_hidden_grad_call(total, sums, grads, gain, e, hidden):
    return pl.pallas_call(
        first_hidden_grad_kernel(total),
        out_shape=jax.ShapeDtypeStruct(hidden.shape, BF16),
        compiler_params=params(),
        name="first_hidden_grad",
    )(sums, grads, gain, e, hidden)


def input_grad_kernel(total):
    def kernel(sums_ref, gain_ref, d_ref, w_ref, e_ref, *refs):
        o_ref = refs[-1]
        _, rs = moments(sums_ref[...], total)
        undo = 1.0 / (gain_ref[...] * rs)
        width = w_ref.shape[0]
        chunk = min(CHUNK, width)
        d = d_ref[...]
        for c in range(0, width, chunk):
            at = slice(c, c + chunk)
            o_ref[:, at] = (
                dot(d, w_ref[at, :], ((1,), (1,))) + e_ref[:, at].astype(F32) * undo[:, at]
            )

    return kernel


def input_grad_call(total, half, sums, gain, d, weight, kept, outs):
    pixels, middle = d.shape
    width = weight.shape[0]
    rows = pixels // STEPS

    def place(b):
        return (2 * half + b, 0)

    return pl.pallas_call(
        input_grad_kernel(total),
        grid=(2,),
        in_specs=[
            pl.BlockSpec((2, width), lambda b: (0, 0)),
            pl.BlockSpec((1, width), lambda b: (0, 0)),
            pl.BlockSpec((rows, middle), place),
            pl.BlockSpec((width, middle), lambda b: (0, 0)),
            pl.BlockSpec((rows, width), place),
        ]
        + [pl.BlockSpec(memory_space=pl.ANY)] * len(outs),
        out_specs=pl.BlockSpec((rows, width), place),
        out_shape=jax.ShapeDtypeStruct((pixels, width), F32),
        input_output_aliases={5: 0} if outs else {},
        compiler_params=params(1),
        name="input_grad",
    )(sums, gain, d, weight, kept, *outs)


def swap(value, mask, count):
    return lax.ppermute(value, AXES, [(i, i ^ mask) for i in range(count)])


ALONG_Z, ALONG_XY, CORES = (8, 16, 24), (2, 4, 6), (1,)


def small_step(value, masks, count):
    arrived = [value] + [swap(value, m, count) for m in masks]
    while len(arrived) > 1:
        arrived = [a + b for a, b in zip(arrived[::2], arrived[1::2])]
    return arrived[0]


def small_sum(value, count, order=(CORES, ALONG_XY, ALONG_Z)):
    if count != 32:
        return lax.psum(value, AXES)
    for masks in order:
        value = small_step(value, masks, count)
    return value


def by_bits(values, place, bits):
    for bit in range(bits):
        paired = values.reshape((1 << (bits - bit - 1), 2, 1 << bit) + values.shape[1:])
        flipped = paired[:, ::-1].reshape(values.shape)
        values = jnp.where(((place >> bit) & 1) == 1, flipped, values)
    return values


def scatter_step(value, stage, index, count):
    shift, bits = stage
    n = 1 << bits
    mine = (index >> shift) & (n - 1)
    parts = value.reshape((n, value.shape[0] // n) + value.shape[1:])
    kept = lax.dynamic_index_in_dim(parts, mine, 0, keepdims=False).astype(F32)
    for m in range(1, n):
        leaving = lax.dynamic_index_in_dim(parts, mine ^ m, 0, keepdims=False)
        kept = kept + swap(leaving, m << shift, count).astype(F32)
    return kept.astype(BF16)


def gather_step(value, stage, index, count):
    shift, bits = stage
    n = 1 << bits
    arrived = [value] + [swap(value, m << shift, count) for m in range(1, n)]
    value = by_bits(jnp.stack(arrived), (index >> shift) & (n - 1), bits)
    return value.reshape((n * value.shape[1],) + value.shape[2:])


STAGES = (((0, 1), (1, 1), (2, 1), (3, 2)), ((0, 1), (2, 1), (1, 1), (3, 2)))


def scatter_steps(halves, step, index, count):
    return [scatter_step(halves[i], STAGES[i][step], index, count) for i in range(2)]


def gather_steps(halves, step, index, count):
    return [gather_step(halves[i], STAGES[i][step], index, count) for i in range(2)]


def body(
    block_in,
    crop_codes,
    tile_perm,
    reduce_weight,
    dilated_weight,
    expand_weight,
    first_gain,
    first_bias,
    middle_gain,
    middle_bias,
    last_gain,
    last_bias,
    cotangent,
):
    devices = lax.axis_size("dp")
    replicas = lax.axis_size("rep")
    count = devices * replicas
    sets = crop_codes.shape[1]
    phases = 16 * sets // devices
    pixels, width = block_in.shape[1:]
    middle = reduce_weight.shape[1]
    tiles = tile_perm.shape[2]
    each = tiles // devices
    total = float(pixels * count)

    place = lax.axis_index("dp").astype(jnp.int32)
    set_index = place * phases // 16
    codes = lax.dynamic_index_in_dim(crop_codes[0], set_index, 0, keepdims=False)
    order = lax.dynamic_index_in_dim(tile_perm[0], set_index, 0, keepdims=False)
    table = tile_table(codes, order, tiles)
    perm = order.reshape(1, tiles)
    parted = (devices, phases * each, middle) if phases > 1 else (1, tiles, middle)

    def exchange(values):
        values = values.reshape(devices, phases * each, middle)
        return lax.all_to_all(values, "dp", split_axis=0, concat_axis=0, tiled=True)

    def to_phases(values):
        return exchange(values).reshape(parted)

    def to_pixels(values):
        return exchange(values).reshape(pixels, middle)

    flat = block_in[0]
    upstream = cotangent[0]
    taps = dilated_weight.reshape(3, 3, middle, middle)
    gain1, bias1 = first_gain.reshape(1, middle), first_bias.reshape(1, middle)
    gain2, bias2 = middle_gain.reshape(1, middle), middle_bias.reshape(1, middle)
    gain3, bias3 = last_gain.reshape(1, width), last_bias.reshape(1, width)

    index = place * replicas + lax.axis_index("rep").astype(jnp.int32)
    tree = count == 32

    def after(value, other):
        return lax.optimization_barrier((value, other)) if tree else (value, other)

    def halves_of(value):
        return [value[: value.shape[0] // 2], value[value.shape[0] // 2 :]]

    def scatter(value, step):
        return scatter_steps(value, step, index, count) if tree else value

    hidden1, part = first_call(flat, reduce_weight)
    slots = to_phases(hidden1)
    sums1 = small_sum(part, count)
    columns, hidden2, part, slots = conv_call(
        total, phases, sums1, gain1, bias1, table, perm, taps, slots
    )
    arrived = to_pixels(slots)
    sums2 = small_sum(part, count)
    act2, part = third_stats_call(total, sums2, gain2, bias2, expand_weight, arrived)
    sums3 = small_sum(part, count)
    block_out, kept, low, part, raw = output_call(
        total, sums3, gain3, bias3, expand_weight, act2, flat, upstream
    )
    if tree:
        part = small_step(part, ALONG_Z, count)
        raw, part = after(raw, part)
    slots = to_phases(raw)
    grads3 = small_sum(part, count, (ALONG_XY, CORES))
    fix = correction_call(
        total, sums3, grads3, gain3, expand_weight, sums2, gain2, bias2, hidden2
    )
    grad3 = third_grad_call(total, sums3, grads3, gain3, expand_weight, act2, kept, low)
    expand_grad = dot(act2, grad3, ((0,), (0,)))
    slots, expand_grad = lax.optimization_barrier((slots, expand_grad))
    e2, part = second_grad_call(
        total, phases, sums2, gain2, bias2, table, perm, hidden2, fix, slots
    )
    grads2 = small_sum(part, count)
    *shifted, slots = conv_grad_call(
        total, phases, sums2, grads2, gain2, table, hidden2, e2, taps, parted
    )
    arrived = to_pixels(slots)
    dilated = halves_of(
        jnp.concatenate(
            [
                dot(columns[:, dy * middle : (dy + 1) * middle], d, ((0,), (0,))).astype(BF16)
                for dy in range(3)
                for d in shifted
            ],
            axis=0,
        )
    )
    arrived, dilated = after(arrived, dilated)
    e1, part = first_grad_call(total, sums1, gain1, bias1, arrived, hidden1)
    dilated = scatter(dilated, 0)
    grads1 = small_sum(part, count)
    grads1, dilated = after(grads1, dilated)
    grad1 = first_hidden_grad_call(total, sums1, grads1, gain1, e1, hidden1)
    dilated = scatter(dilated, 1)
    reduced = halves_of(dot(flat, grad1, ((0,), (0,))).astype(BF16))
    reduced, dilated = after(reduced, dilated)
    reduced = scatter(reduced, 0)
    grad1, dilated = after(grad1, dilated)
    grad_in = input_grad_call(total, 0, sums3, gain3, grad1, reduce_weight, kept, [])
    dilated = scatter(dilated, 2)
    (grad1, grad_in), (dilated, reduced) = after((grad1, grad_in), (dilated, reduced))
    grad_in = input_grad_call(total, 1, sums3, gain3, grad1, reduce_weight, kept, [grad_in])
    dilated = scatter(dilated, 3)
    reduced = scatter(reduced, 1)
    reduced, grad_in = after(reduced, grad_in)
    for step in (2, 3):
        reduced = scatter(reduced, step)
    expand_grad = lax.psum(expand_grad, AXES)
    if tree:
        for step in (3, 2, 1, 0):
            dilated = gather_steps(dilated, step, index, count)
            if step == 1:
                dilated, expand_grad = after(dilated, expand_grad)
            reduced = gather_steps(reduced, step, index, count)
    dilated_grad = jnp.concatenate(dilated, axis=0).astype(F32)
    reduce_grad = jnp.concatenate(reduced, axis=0).astype(F32)
    if not tree:
        dilated_grad, reduce_grad = lax.psum((dilated_grad, reduce_grad), AXES)
    return (
        block_out.reshape(1, pixels, width),
        grad_in.reshape(1, pixels, width),
        reduce_grad,
        dilated_grad,
        expand_grad,
        grads1[1],
        grads1[0],
        grads2[1],
        grads2[0],
        grads3[1],
        grads3[0],
    )


def solution(mesh):
    in_specs = (
        P("rep", "dp", None),
        P("rep", None, None),
        P("rep", None, None),
        P(),
        P(),
        P(),
        P(),
        P(),
        P(),
        P(),
        P(),
        P(),
        P("rep", "dp", None),
    )
    out_specs = (P("rep", "dp", None),) * 2 + (P(),) * 9
    return jax.shard_map(body, mesh=mesh, in_specs=in_specs, out_specs=out_specs, check_vma=False)
```
